32 devices in a mesh: groups: 2 (over x), ctx: 16 (over z, y, core).
Axes of the slice: x: 2, y: 2, z: 4, core: 2. Of those that a mesh axis runs over, the one named last changes fastest.
Arguments:
- tokens: bfloat16 [32, 8192], P('groups', 'ctx'), parts along dimension 0, may hold values from -6 to 6
- attn_gain: float32 [8192], replicated, may hold values from 0.1 to 1.9
- mlp_gain: float32 [8192], replicated, may hold values from 0.1 to 1.9
- q_weight: bfloat16 [8192, 8192], P(None, 'ctx'), may hold values from -0.0625 to 0.0625
- k_weight: bfloat16 [8192, 1024], P('ctx'), may hold values from -0.5 to 0.5
- v_weight: bfloat16 [8192, 1024], P('ctx'), may hold values from -0.0625 to 0.0625
- o_weight: bfloat16 [8192, 8192], P(None, 'ctx'), may hold values from -0.0625 to 0.0625
- gate_weight: bfloat16 [8192, 16384], P(None, 'ctx'), may hold values from -0.0625 to 0.0625
- up_weight: bfloat16 [8192, 16384], P(None, 'ctx'), may hold values from -0.0625 to 0.0625
- down_weight: bfloat16 [16384, 8192], P('ctx'), may hold values from -0.046875 to 0.046875
- prefix_keys: bfloat16 [8192, 1024], P(('groups', 'ctx')), parts along dimension 0, may hold values from -400 to 400
- prefix_values: bfloat16 [8192, 1024], P(('groups', 'ctx')), parts along dimension 0, may hold values from -36 to 36
- suffix_keys: bfloat16 [256, 16, 1024], P(('groups', 'ctx')), parts along dimension 0, may hold values from -18 to 18
- suffix_values: bfloat16 [256, 16, 1024], P(('groups', 'ctx')), parts along dimension 0, may hold values from -18 to 18
- suffix_lengths: int32 [32], P('groups'), parts along dimension 0, may hold values from 1 to 128, as said below
- suffix_table: int32 [32, 8], P(('groups', 'ctx')), parts along dimension 0, may hold values from 0 to 7, as said below
Outputs:
- layer_out: bfloat16 [32, 8192], P('groups', 'ctx'), parts along dimension 0
The draws below stay inside these ranges and needn't reach their ends.
There are 2 independent parts, one for each index of `groups`. The reference program is written for one: setup_inputs(seed, part) draws one part's arguments, and reference() takes and returns one part's arrays. A program takes and returns all parts, laid end to end along the dimension named above; an argument that names none is the same for every part. Nothing has to cross between parts.
Inputs may be any that keep to these rules, and one draw needn't show every extreme that they name: `suffix_lengths`: at most 128; some sample has exactly 128. `suffix_table`: in every aligned block of 1 row, the entries name each of 0 to 7 exactly once.
All inputs are finite; a program needn't handle non-finite values.
Results may differ from the reference program's by a relative error of at most 0.014.
The reference program's roundings to bfloat16 on the way (of `attn_normed`, `queries`, `fresh_keys`, `fresh_values`, `attention`, `mixed`, `mlp_normed` and `hidden`) count: a program that leaves them out, or rounds other values in their place, can miss the bound.
Values may be sent and summed in bfloat16 or wider, within the bound.
A program may use at most 128 MiB of HBM per device.

```python
import math
import jax
import jax.numpy as jnp
from jax import lax

D = 8192
HEADS = 64
KV_HEADS = 8
HEAD_DIM = 128
FFW = 16384
S_DEV = 1
BLK = 16
MAXB = 8
QW = 8192
KVW = 1024
S = 16
PRE = 4096
POOL = 128


def draw_suffix_lengths(key, part):
    suffix_span = MAXB * BLK
    lengths = jax.random.randint(key, (S,), 1, suffix_span + 1, dtype=jnp.int32)
    chosen = jax.random.randint(jax.random.fold_in(key, 11), (), 0, S, dtype=jnp.int32)
    return lengths.at[chosen].set(suffix_span)


def draw_suffix_table(key, part):
    device_count = S // S_DEV
    device_keys = jax.random.split(key, device_count)
    orders = jax.vmap(lambda single: jax.random.permutation(single, S_DEV * MAXB))(device_keys)
    return orders.astype(jnp.int32).reshape(S, MAXB)


def draw_prefix_keys(key, part):
    key_width = KV_HEADS * HEAD_DIM
    base = jnp.clip(jax.random.normal(key, (PRE, key_width), jnp.float32), -6.0, 6.0)
    return base.astype(jnp.bfloat16)


def block_levels(own_key, dims, pieces, least, largest):
    def one(axis_at, blocks):
        steps = jax.random.uniform(jax.random.fold_in(jax.random.fold_in(own_key, 6), axis_at), (blocks,), jnp.float32, least / len(pieces), largest / len(pieces))
        return jnp.repeat(jnp.exp(steps), dims[axis_at] // blocks).reshape((-1,) + (1,) * (len(dims) - axis_at - 1))

    level = one(*pieces[0])
    for cut in pieces[1:]:
        level = level * one(*cut)
    return level


def normal_values(stream_key, extent, width, reach, pieces=(), kind=jnp.bfloat16):
    result = width * jax.random.normal(stream_key, extent, jnp.float32)
    if pieces:
        result = result * block_levels(stream_key, extent, pieces, -0.22, 0.18)
    return jnp.clip(result, -reach, reach).astype(kind)


def setup_inputs(seed: int = 0, part: int = 0) -> dict:
    keys = jax.random.split(jax.random.key(seed), 17)
    part_splits = jax.random.split(jax.random.fold_in(keys[16], part), 17)
    tokens = normal_values(part_splits[0], (S, D), 1.0, 6.0, ((1, 16),))
    attn_gain = jnp.clip(1.0 + 0.18 * jax.random.normal(keys[1], (D,), jnp.float32), 0.1, 1.9)
    mlp_gain = jnp.clip(1.0 + 0.18 * jax.random.normal(keys[2], (D,), jnp.float32), 0.1, 1.9)
    q_weight = normal_values(keys[3], (D, QW), D ** -0.5, 0.0625, ((1, 16),))
    k_weight = normal_values(keys[4], (D, KVW), (D // 64) ** -0.5, 0.5, ((0, 16),))
    v_weight = normal_values(keys[5], (D, KVW), D ** -0.5, 0.0625, ((0, 16),))
    o_weight = normal_values(keys[6], (QW, D), QW ** -0.5, 0.0625, ((1, 16),))
    gate_weight = normal_values(keys[7], (D, FFW), D ** -0.5, 0.0625, ((1, 16),))
    up_weight = normal_values(keys[8], (D, FFW), D ** -0.5, 0.0625, ((1, 16),))
    down_weight = normal_values(keys[9], (FFW, D), FFW ** -0.5, 0.046875, ((0, 16),))
    prefix_keys = draw_prefix_keys(jax.random.fold_in(jax.random.fold_in(keys[16], part), 71), part)
    prefix_values = normal_values(part_splits[11], (PRE, KVW), 6.0, 36.0, ((0, 16),))
    suffix_keys = normal_values(part_splits[12], (POOL, BLK, KVW), 3.0, 18.0, ((0, 16),))
    suffix_values = normal_values(part_splits[13], (POOL, BLK, KVW), 3.0, 18.0, ((0, 16),))
    suffix_lengths = draw_suffix_lengths(jax.random.fold_in(jax.random.fold_in(keys[16], part), 71), part)
    suffix_table = draw_suffix_table(jax.random.fold_in(jax.random.fold_in(keys[16], part), 71), part)
    return {"tokens": tokens, "attn_gain": attn_gain, "mlp_gain": mlp_gain, "q_weight": q_weight, "k_weight": k_weight, "v_weight": v_weight, "o_weight": o_weight, "gate_weight": gate_weight, "up_weight": up_weight, "down_weight": down_weight, "prefix_keys": prefix_keys, "prefix_values": prefix_values, "suffix_keys": suffix_keys, "suffix_values": suffix_values, "suffix_lengths": suffix_lengths, "suffix_table": suffix_table}


EPSILON = 1e-05
ROPE_BASE = 500000.0

def rms_rows(matrix, gain_vector):
    widened = matrix.astype(jnp.float32)
    mean_square = lax.optimization_barrier(jnp.mean(widened * widened, axis=-1, keepdims=True))
    return (widened * lax.rsqrt(mean_square + EPSILON) * gain_vector).astype(jnp.bfloat16)

def rotate(matrix, position, columns):
    pair_index = (columns % HEAD_DIM // 2).astype(jnp.float32)
    frequency = jnp.exp(pair_index * (-2.0 * math.log(ROPE_BASE) / HEAD_DIM))
    angles = position.astype(jnp.float32)[:, None] * frequency[None, :]
    cosine = jnp.cos(angles[:, 0::2])
    sine_part = jnp.sin(angles[:, 0::2])
    even_part = matrix[:, 0::2]
    odd_part = matrix[:, 1::2]
    rotated_even = even_part * cosine - odd_part * sine_part
    rotated_odd = even_part * sine_part + odd_part * cosine
    return jnp.stack([rotated_even, rotated_odd], axis=-1).reshape(matrix.shape)

def reference(tokens, attn_gain, mlp_gain, q_weight, k_weight, v_weight, o_weight, gate_weight, up_weight, down_weight, prefix_keys, prefix_values, suffix_keys, suffix_values, suffix_lengths, suffix_table):
    samples = tokens.shape[0]
    group_size = HEADS // KV_HEADS
    score_scale = 1.0 / math.sqrt(HEAD_DIM)
    position = PRE + suffix_lengths
    attn_normed = rms_rows(tokens, attn_gain)
    query_cols = jnp.arange(HEADS * HEAD_DIM, dtype=jnp.int32)
    key_cols = jnp.arange(KV_HEADS * HEAD_DIM, dtype=jnp.int32)
    queries = rotate(jnp.dot(attn_normed, q_weight, preferred_element_type=jnp.float32), position, query_cols).astype(jnp.bfloat16)
    fresh_keys = rotate(jnp.dot(attn_normed, k_weight, preferred_element_type=jnp.float32), position, key_cols).astype(jnp.bfloat16)
    fresh_values = jnp.dot(attn_normed, v_weight, preferred_element_type=jnp.float32).astype(jnp.bfloat16)
    query_heads = queries.reshape(samples, KV_HEADS, group_size, HEAD_DIM).astype(jnp.float32)
    grouped = query_heads.transpose(1, 0, 2, 3)
    head_keys = prefix_keys.reshape(PRE, KV_HEADS, HEAD_DIM).astype(jnp.float32).transpose(1, 0, 2)
    head_values = prefix_values.reshape(PRE, KV_HEADS, HEAD_DIM).astype(jnp.float32).transpose(1, 0, 2)

    def prefix_head(operands):
        query_block, key_block, value_block = operands
        scores = jnp.einsum('sgd,td->sgt', query_block, key_block) * score_scale
        peak_block = lax.optimization_barrier(jnp.max(scores, axis=-1))
        weights = jnp.exp(scores - peak_block[..., None])
        total_block = lax.optimization_barrier(jnp.sum(weights, axis=-1))
        rounded = lax.optimization_barrier(weights.astype(jnp.bfloat16)).astype(jnp.float32)
        summed = jnp.einsum('sgt,td->sgd', rounded, value_block)
        return (peak_block, total_block, summed)
    peak_heads, total_heads, sum_heads = lax.map(prefix_head, (grouped, head_keys, head_values))
    prefix_peak = peak_heads.transpose(1, 0, 2).reshape(samples, HEADS)
    prefix_total = total_heads.transpose(1, 0, 2).reshape(samples, HEADS)
    prefix_sum = sum_heads.transpose(1, 0, 2, 3).reshape(samples, HEADS, HEAD_DIM)
    owner_base = jnp.arange(samples, dtype=jnp.int32) // S_DEV * (S_DEV * MAXB)
    blocks = owner_base[:, None] + suffix_table
    suffix_span = MAXB * BLK
    owned_keys = suffix_keys[blocks].reshape(samples, suffix_span, KV_HEADS, HEAD_DIM)
    owned_values = suffix_values[blocks].reshape(samples, suffix_span, KV_HEADS, HEAD_DIM)
    every_key = jnp.concatenate([owned_keys, fresh_keys.reshape(samples, 1, KV_HEADS, HEAD_DIM)], axis=1).astype(jnp.float32)
    every_value = jnp.concatenate([owned_values, fresh_values.reshape(samples, 1, KV_HEADS, HEAD_DIM)], axis=1).astype(jnp.float32)
    slot_index = jnp.arange(suffix_span + 1, dtype=jnp.int32)
    live_mask = (slot_index[None, :] < suffix_lengths[:, None]) | (slot_index[None, :] == suffix_span)
    suffix_scores = jnp.einsum('sngd,sjnd->sngj', query_heads, every_key) * score_scale
    suffix_scores = jnp.where(live_mask[:, None, None, :], suffix_scores, -1e+30)
    suffix_peak = lax.optimization_barrier(jnp.max(suffix_scores, axis=-1))
    suffix_weights = jnp.exp(suffix_scores - suffix_peak[..., None])
    suffix_total = lax.optimization_barrier(jnp.sum(suffix_weights, axis=-1)).reshape(samples, HEADS)
    suffix_rounded = lax.optimization_barrier(suffix_weights.astype(jnp.bfloat16)).astype(jnp.float32)
    suffix_sum = jnp.einsum('sngj,sjnd->sngd', suffix_rounded, every_value).reshape(samples, HEADS, HEAD_DIM)
    suffix_peak = suffix_peak.reshape(samples, HEADS)
    peak_all = jnp.maximum(prefix_peak, suffix_peak)
    prefix_factor = jnp.exp(prefix_peak - peak_all)
    suffix_factor = jnp.exp(suffix_peak - peak_all)
    numerator = prefix_sum * prefix_factor[..., None] + suffix_sum * suffix_factor[..., None]
    denominator = prefix_total * prefix_factor + suffix_total * suffix_factor
    attention = (numerator / denominator[..., None]).reshape(samples, HEADS * HEAD_DIM).astype(jnp.bfloat16)
    mixed = (tokens.astype(jnp.float32) + jnp.dot(attention, o_weight, preferred_element_type=jnp.float32)).astype(jnp.bfloat16)
    mlp_normed = rms_rows(mixed, mlp_gain)
    gate_proj = jnp.dot(mlp_normed, gate_weight, preferred_element_type=jnp.float32)
    up_proj = jnp.dot(mlp_normed, up_weight, preferred_element_type=jnp.float32)
    hidden = (jax.nn.silu(gate_proj) * up_proj).astype(jnp.bfloat16)
    layer_out = mixed.astype(jnp.float32) + jnp.dot(hidden, down_weight, preferred_element_type=jnp.float32)
    return layer_out.astype(jnp.bfloat16)
```

```python
import functools
import math

import jax
import jax.numpy as jnp
from jax import lax
from jax.experimental import pallas as pl
from jax.experimental.pallas import tpu as pltpu
from jax.sharding import PartitionSpec as P

HEADS = 64
KV_HEADS = 8
HEAD_DIM = 128


EPSILON = 1e-05
ROPE_BASE = 500000.0


def rotate(matrix, position, columns):
    pair_index = (columns % HEAD_DIM // 2).astype(jnp.float32)
    frequency = jnp.exp(pair_index * (-2.0 * math.log(ROPE_BASE) / HEAD_DIM))
    angles = position.astype(jnp.float32)[:, None] * frequency[None, :]
    cosine = jnp.cos(angles[:, 0::2])
    sine_part = jnp.sin(angles[:, 0::2])
    even_part = matrix[:, 0::2]
    odd_part = matrix[:, 1::2]
    rotated_even = even_part * cosine - odd_part * sine_part
    rotated_odd = even_part * sine_part + odd_part * cosine
    return jnp.stack([rotated_even, rotated_odd], axis=-1).reshape(matrix.shape)


def normalized_rows(shard_rows, gain_vector):
    self_index = lax.axis_index("ctx")
    feature_width = shard_rows.shape[1]
    gathered_raw = lax.all_gather(shard_rows, "ctx", axis=1, tiled=True)
    widened = gathered_raw.astype(jnp.float32)
    mean_square = jnp.mean(widened * widened, axis=1, keepdims=True)
    gathered = (widened * lax.rsqrt(mean_square + EPSILON) * gain_vector).astype(jnp.bfloat16)
    local_part = lax.dynamic_slice_in_dim(gathered, self_index * feature_width, feature_width, 1)
    return (gathered, local_part)


def plain_body(
    tokens,
    attn_gain,
    mlp_gain,
    q_weight,
    k_weight,
    v_weight,
    o_weight,
    gate_weight,
    up_weight,
    down_weight,
    prefix_keys,
    prefix_values,
    suffix_keys,
    suffix_values,
    suffix_lengths,
    suffix_table,
):
    self_index = lax.axis_index("ctx")
    devices = lax.axis_size("ctx")
    samples = tokens.shape[0]
    own_rows = suffix_table.shape[0]
    group_size = HEADS // KV_HEADS
    score_scale = 1.0 / math.sqrt(HEAD_DIM)
    prefix_rows = prefix_keys.shape[0]
    row_start = self_index * own_rows
    position = prefix_rows * devices + suffix_lengths
    own_position = lax.dynamic_slice_in_dim(position, row_start, own_rows, 0)
    own_lengths = lax.dynamic_slice_in_dim(suffix_lengths, row_start, own_rows, 0)
    attn_normed, local_normed = normalized_rows(tokens, attn_gain)
    query_width = q_weight.shape[1]
    query_cols = self_index * query_width + jnp.arange(query_width, dtype=jnp.int32)
    query_part = rotate(
        jnp.dot(attn_normed, q_weight, preferred_element_type=jnp.float32), position, query_cols
    ).astype(jnp.bfloat16)
    queries = lax.all_gather(query_part, "ctx", axis=1, tiled=True)
    key_width = k_weight.shape[1]
    key_term = jnp.dot(local_normed, k_weight, preferred_element_type=jnp.float32)
    value_term = jnp.dot(local_normed, v_weight, preferred_element_type=jnp.float32)
    fresh = lax.psum_scatter(
        jnp.concatenate([key_term, value_term], axis=1), "ctx", scatter_dimension=0, tiled=True
    )
    fresh_keys = rotate(
        fresh[:, :key_width], own_position, jnp.arange(key_width, dtype=jnp.int32)
    ).astype(jnp.bfloat16)
    fresh_values = fresh[:, key_width:].astype(jnp.bfloat16)
    query_heads = queries.reshape(samples, KV_HEADS, group_size, HEAD_DIM)
    head_keys = prefix_keys.reshape(prefix_rows, KV_HEADS, HEAD_DIM)
    head_values = prefix_values.reshape(prefix_rows, KV_HEADS, HEAD_DIM)
    scores = (
        jnp.einsum("sngd,tnd->sngt", query_heads, head_keys, preferred_element_type=jnp.float32)
        * score_scale
    )
    local_peak = jnp.max(scores, axis=-1)
    peak_heads = lax.pmax(local_peak, "ctx")
    weights = jnp.exp(scores - peak_heads[..., None])
    partial_total = jnp.sum(weights, axis=-1).reshape(samples, HEADS)
    summed = jnp.einsum(
        "sngt,tnd->sngd",
        weights.astype(jnp.bfloat16),
        head_values,
        preferred_element_type=jnp.float32,
    ).reshape(samples, HEADS * HEAD_DIM)
    every_sum, every_total = lax.psum((summed, partial_total), "ctx")
    prefix_sum = lax.dynamic_slice_in_dim(every_sum, row_start, own_rows, 0)
    prefix_total = lax.dynamic_slice_in_dim(every_total, row_start, own_rows, 0)
    prefix_peak = lax.dynamic_slice_in_dim(
        peak_heads.reshape(samples, HEADS), row_start, own_rows, 0
    )
    prefix_sum = prefix_sum.reshape(own_rows, HEADS, HEAD_DIM)
    own_queries = lax.dynamic_slice_in_dim(query_heads, row_start, own_rows, 0)
    suffix_span = suffix_table.shape[1] * suffix_keys.shape[1]
    owned_keys = suffix_keys[suffix_table].reshape(own_rows, suffix_span, KV_HEADS, HEAD_DIM)
    owned_values = suffix_values[suffix_table].reshape(own_rows, suffix_span, KV_HEADS, HEAD_DIM)
    every_key = jnp.concatenate(
        [owned_keys, fresh_keys.reshape(own_rows, 1, KV_HEADS, HEAD_DIM)], axis=1
    )
    every_value = jnp.concatenate(
        [owned_values, fresh_values.reshape(own_rows, 1, KV_HEADS, HEAD_DIM)], axis=1
    )
    slot_index = jnp.arange(suffix_span + 1, dtype=jnp.int32)
    live_mask = (slot_index[None, :] < own_lengths[:, None]) | (slot_index[None, :] == suffix_span)
    suffix_scores = (
        jnp.einsum("sngd,sjnd->sngj", own_queries, every_key, preferred_element_type=jnp.float32)
        * score_scale
    )
    suffix_scores = jnp.where(live_mask[:, None, None, :], suffix_scores, -1e30)
    suffix_peak = jnp.max(suffix_scores, axis=-1)
    suffix_weights = jnp.exp(suffix_scores - suffix_peak[..., None])
    suffix_total = jnp.sum(suffix_weights, axis=-1).reshape(own_rows, HEADS)
    suffix_sum = jnp.einsum(
        "sngj,sjnd->sngd",
        suffix_weights.astype(jnp.bfloat16),
        every_value,
        preferred_element_type=jnp.float32,
    ).reshape(own_rows, HEADS, HEAD_DIM)
    suffix_peak = suffix_peak.reshape(own_rows, HEADS)
    peak_all = jnp.maximum(prefix_peak, suffix_peak)
    prefix_factor = jnp.exp(prefix_peak - peak_all)
    suffix_factor = jnp.exp(suffix_peak - peak_all)
    numerator = prefix_sum * prefix_factor[..., None] + suffix_sum * suffix_factor[..., None]
    denominator = prefix_total * prefix_factor + suffix_total * suffix_factor
    attention = (
        (numerator / denominator[..., None])
        .reshape(own_rows, HEADS * HEAD_DIM)
        .astype(jnp.bfloat16)
    )
    attended = jnp.dot(
        lax.all_gather(attention, "ctx", axis=0, tiled=True),
        o_weight,
        preferred_element_type=jnp.float32,
    )
    mixed_rows = (tokens.astype(jnp.float32) + attended).astype(jnp.bfloat16)
    mlp_normed = normalized_rows(mixed_rows, mlp_gain)[0]
    gate_proj = jnp.dot(mlp_normed, gate_weight, preferred_element_type=jnp.float32)
    up_proj = jnp.dot(mlp_normed, up_weight, preferred_element_type=jnp.float32)
    hidden = (jax.nn.silu(gate_proj) * up_proj).astype(jnp.bfloat16)
    partial_value = jnp.dot(hidden, down_weight, preferred_element_type=jnp.float32)
    shares = lax.psum_scatter(partial_value, "ctx", scatter_dimension=1, tiled=True)
    return (mixed_rows.astype(jnp.float32) + shares).astype(jnp.bfloat16)


TOK, QRY, FRESH, PART, STAT, ATT, MIX, DOWN, PHASES = range(9)
LANES = HEAD_DIM
GROUP = HEADS // KV_HEADS
FITS = 16


def regroup(rows, inner, outer):
    row = lax.broadcasted_iota(jnp.int32, (rows, rows), 0)
    column = lax.broadcasted_iota(jnp.int32, (rows, rows), 1)
    picked = (row % outer) * inner + row // outer
    return jnp.where(column == picked, 1.0, 0.0).astype(jnp.bfloat16)


def turn(block, cosine, signed_sine, even):
    swapped = jnp.where(even, pltpu.roll(block, LANES - 1, 1), pltpu.roll(block, 1, 1))
    return block * cosine + swapped * signed_sine


def layer_kernel(
    n,
    prefix_tokens,
    tokens,
    attn_gain,
    mlp_gain,
    q_hbm,
    k_hbm,
    v_hbm,
    o_hbm,
    gate_hbm,
    up_hbm,
    down_hbm,
    pk_hbm,
    pv_hbm,
    sk_hbm,
    sv_hbm,
    lengths,
    table,
    out,
    qw,
    kw,
    vw,
    ow,
    gw,
    uw,
    dw,
    pk,
    pv,
    sk,
    sv,
    again,
    mgain,
    tokbuf,
    qbuf,
    qperm,
    psend,
    precv,
    ssend,
    srecv,
    fsend,
    frecv,
    attbuf,
    attl,
    mixbuf,
    dsend,
    drecv,
    load_sem,
    big_sem,
    send_sem,
    recv_sem,
):
    me = lax.axis_index("ctx")
    partner = me + 1 - 2 * (me % 2)
    half = n // 2
    samples, width = tokens.shape
    ffn = gw.shape[1]
    scale = 1.0 / math.sqrt(HEAD_DIM)
    f32, bf16 = jnp.float32, jnp.bfloat16

    def load(source, target, index):
        return pltpu.make_async_copy(source, target, load_sem.at[index])

    def rows_of(d):
        return pl.ds(pl.multiple_of(d * width, width), width)

    def chunk(kind, d):
        if kind == 0:
            return pltpu.make_async_copy(q_hbm.at[rows_of(d)], qw.at[rows_of(d)], big_sem.at[0, d])
        if kind == 1:
            return pltpu.make_async_copy(o_hbm.at[rows_of(d)], ow.at[rows_of(d)], big_sem.at[1, d])
        if kind == 2:
            return pltpu.make_async_copy(
                gate_hbm.at[rows_of(d)], gw.at[rows_of(d)], big_sem.at[2, d]
            )
        return pltpu.make_async_copy(up_hbm.at[rows_of(d)], uw.at[rows_of(d)], big_sem.at[3, d])

    def down_chunk(step, target, place):
        d = (me + 1 + step) % n
        return pltpu.make_async_copy(
            down_hbm.at[:, rows_of(d)],
            target.at[pl.ds(pl.multiple_of(place * ffn, ffn), ffn)],
            big_sem.at[4, step],
        )

    def remote(phase, source, target, slot, landed, device):
        return pltpu.make_async_remote_copy(
            src_ref=source,
            dst_ref=target,
            send_sem=send_sem.at[phase, slot],
            recv_sem=recv_sem.at[phase, landed],
            device_id={"ctx": device},
            device_id_type=pl.DeviceIdType.MESH,
        )

    def loop(low, high, step):
        def wrapped(index, carry):
            step(index)
            return carry

        lax.fori_loop(low, high, wrapped, 0)

    def spread(phase, buf):
        loop(
            1,
            half,
            lambda k: remote(
                phase, buf.at[me], buf.at[me], k, me, (me + 2 * k) % n
            ).start(),
        )
        remote(phase, buf.at[me], buf.at[me], 0, me, partner).start()

    def collect(phase, buf):
        def relay(k):
            origin = (me + n - 2 * k) % n
            remote(phase, buf.at[origin], buf.at[origin], 0, origin, partner).wait_recv()
            remote(phase, buf.at[origin], buf.at[origin], half + k, origin, partner).start()

        def arrive(k):
            origin = (partner + n - 2 * k) % n
            remote(phase, buf.at[origin], buf.at[origin], 0, origin, partner).wait_recv()

        loop(1, half, relay)
        loop(0, half, arrive)

    def drain(phase, buf):
        def one(k):
            remote(phase, buf.at[me], buf.at[me], k, me, partner).wait_send()

        loop(0, half, one)
        loop(half + 1, n, one)

    def scatter_one(phase, source, target, k):
        device = (me + k) % n
        remote(phase, source.at[device], target.at[me], k, me, device).start()

    def gather_one(phase, source, target, k):
        origin = (me + n - k) % n
        remote(phase, source.at[origin], target.at[origin], k, origin, origin).wait_recv()

    def sent_one(phase, source, target, k):
        device = (me + k) % n
        remote(phase, source.at[device], target.at[me], k, me, device).wait_send()

    first = load(tokens, tokbuf.at[me], 0)
    first.start()
    small = [
        load(attn_gain, again, 1),
        load(mlp_gain, mgain, 2),
        load(k_hbm, kw, 3),
        load(v_hbm, vw, 4),
        load(pk_hbm, pk, 5),
        load(pv_hbm, pv, 6),
        load(sk_hbm, sk, 7),
        load(sv_hbm, sv, 8),
    ]
    barrier = pltpu.get_barrier_semaphore()
    loop(
        1,
        n,
        lambda k: pl.semaphore_signal(
            barrier,
            inc=1,
            device_id={"ctx": (me + k) % n},
            device_id_type=pl.DeviceIdType.MESH,
        ),
    )
    small[0].start()
    loop(0, n, lambda d: chunk(0, d).start())
    for copy in small[1:]:
        copy.start()
    first.wait()
    pl.semaphore_wait(barrier, n - 1)
    spread(TOK, tokbuf)
    loop(0, n, lambda d: chunk(1, d).start())

    def start_pair(d):
        chunk(2, d).start()
        chunk(3, d).start()

    loop(0, n, start_pair)
    loop(0, half, lambda i: down_chunk(i, dw, i).start())

    lane = lax.broadcasted_iota(jnp.int32, (samples, LANES), 1)
    row = lax.broadcasted_iota(jnp.int32, (samples, LANES), 0)
    even = lane % 2 == 0
    pair_index = (lane // 2).astype(f32)
    frequency = jnp.exp(pair_index * (-2.0 * math.log(ROPE_BASE) / HEAD_DIM))
    position = jnp.zeros((samples, LANES), jnp.int32)
    for s in range(samples):
        position = jnp.where(row == s, lengths[s] + prefix_tokens, position)
    angles = position.astype(f32) * frequency
    cosine = jnp.cos(angles)
    sine = jnp.where(even, -1.0, 1.0) * jnp.sin(angles)
    own_length = lengths[me]
    own_angles = (own_length + prefix_tokens).astype(f32) * frequency
    own_cosine = jnp.cos(own_angles)[:KV_HEADS]
    own_sine = (jnp.where(even, -1.0, 1.0) * jnp.sin(own_angles))[:KV_HEADS]
    to_sample = regroup(samples * GROUP, samples, GROUP)
    square = regroup(samples * samples, samples, samples)

    def inverse_root(buf):
        def add(d, total):
            block = buf[d].astype(f32)
            return total + jnp.sum(block * block, axis=1, keepdims=True)

        total = lax.fori_loop(0, n, add, jnp.zeros((samples, 1), f32))
        return lax.rsqrt(total / (n * width) + EPSILON)

    def normed(buf, root, gain, d):
        return (buf[d].astype(f32) * root * gain[:, rows_of(d)]).astype(bf16)

    for copy in small[:2]:
        copy.wait()
    collect(TOK, tokbuf)
    root = inverse_root(tokbuf)

    def q_step(d, total):
        chunk(0, d).wait()
        return total + jnp.dot(
            normed(tokbuf, root, again, d), qw[rows_of(d), :], preferred_element_type=f32
        )

    query = lax.fori_loop(0, n, q_step, jnp.zeros((samples, width), f32))
    for j in range(width // LANES):
        piece = slice(j * LANES, (j + 1) * LANES)
        qbuf[me, :, piece] = turn(query[:, piece], cosine, sine, even).astype(bf16)
    spread(QRY, qbuf)
    loop(half, n, lambda i: down_chunk(i, qw, i - half).start())

    for copy in small[2:]:
        copy.wait()
    mine = normed(tokbuf, root, again, me)
    terms = [
        jnp.dot(mine, kw[...], preferred_element_type=f32),
        jnp.dot(mine, vw[...], preferred_element_type=f32),
    ]
    stacked = jnp.concatenate(
        [
            term[:, c * LANES : (c + 1) * LANES]
            for term in terms
            for c in range(KV_HEADS)
        ],
        axis=0,
    )
    upper = stacked.astype(bf16)
    lower = (stacked - upper.astype(f32)).astype(bf16)
    by_owner = jnp.dot(square, upper, preferred_element_type=f32) + jnp.dot(
        square, lower, preferred_element_type=f32
    )
    by_owner = by_owner.reshape(n, 2 * KV_HEADS, LANES)
    fsend[...] = by_owner
    loop(1, n, lambda k: scatter_one(FRESH, fsend, frecv, k))
    frecv[me] = fsend[me]

    collect(QRY, qbuf)
    stat_lane = lax.broadcasted_iota(jnp.int32, (samples * GROUP, LANES), 1)
    stats = jnp.zeros((samples * GROUP, LANES), f32)
    per_device = width // LANES
    held = []
    for k in range(KV_HEADS):
        piece = slice(k * LANES, (k + 1) * LANES)
        heads = [k * GROUP + g for g in range(GROUP)]
        raw = jnp.concatenate(
            [
                qbuf[h // per_device, :, (h % per_device) * LANES : (h % per_device + 1) * LANES]
                for h in heads
            ],
            axis=0,
        )
        arranged = jnp.dot(to_sample, raw, preferred_element_type=f32)
        qperm[k] = arranged
        scores = (
            lax.dot_general(
                arranged.astype(bf16),
                pk[:, piece],
                (((1,), (1,)), ((), ())),
                preferred_element_type=f32,
            )
            * scale
        )
        peak = jnp.max(scores, axis=1, keepdims=True)
        weights = jnp.exp(scores - peak)
        total = jnp.sum(weights, axis=1, keepdims=True)
        summed = jnp.dot(weights.astype(bf16), pv[:, piece], preferred_element_type=f32)
        stats = jnp.where(stat_lane == k, peak, stats)
        stats = jnp.where(stat_lane == k + LANES // 2, total, stats)
        held.append(summed.reshape(samples, GROUP, LANES))
        if k % 2 == 1:
            psend[:, (k - 1) * GROUP : (k + 1) * GROUP, :] = jnp.concatenate(
                held, axis=1
            ).astype(bf16)
            held = []
    ssend[...] = stats.reshape(samples, GROUP, LANES)

    def send_part(k):
        scatter_one(STAT, ssend, srecv, k)
        scatter_one(PART, psend, precv, k)

    loop(1, n, send_part)
    srecv[me] = ssend[me]
    precv[me] = psend[me]

    loop(1, n, lambda k: gather_one(FRESH, fsend, frecv, k))
    fresh = lax.fori_loop(
        0, n, lambda d, total: total + frecv[d], jnp.zeros((2 * KV_HEADS, LANES), f32)
    )
    fresh_keys = (
        turn(fresh[:KV_HEADS], own_cosine, own_sine, even[:KV_HEADS]).astype(bf16).astype(f32)
    )
    fresh_values = fresh[KV_HEADS:].astype(bf16).astype(f32)
    blocks, block = sk.shape[0], sk.shape[1]
    span = blocks * block
    place = lax.broadcasted_iota(jnp.int32, (GROUP, span), 1)
    slot = jnp.zeros((GROUP, span), jnp.int32)
    for i in range(blocks):
        slot = jnp.where(place // block == table[0, i], i * block + place % block, slot)
    live = slot < own_length
    own_lane = lax.broadcasted_iota(jnp.int32, (GROUP, LANES), 1)
    own_peaks = jnp.zeros((GROUP, LANES), f32)
    own_totals = jnp.zeros((GROUP, LANES), f32)
    own_sums = []
    for k in range(KV_HEADS):
        piece = slice(k * LANES, (k + 1) * LANES)
        mine_q = qperm[k, pl.ds(pl.multiple_of(me * GROUP, GROUP), GROUP), :]
        scores = (
            lax.dot_general(
                mine_q.astype(bf16),
                sk[:, :, piece].reshape(span, LANES),
                (((1,), (1,)), ((), ())),
                preferred_element_type=f32,
            )
            * scale
        )
        scores = jnp.where(live, scores, -1e30)
        fresh_score = (
            jnp.sum(mine_q * fresh_keys[k : k + 1], axis=1, keepdims=True) * scale
        )
        peak = jnp.maximum(jnp.max(scores, axis=1, keepdims=True), fresh_score)
        weights = jnp.where(live, jnp.exp(scores - peak), 0.0)
        fresh_weight = jnp.exp(fresh_score - peak)
        total = jnp.sum(weights, axis=1, keepdims=True) + fresh_weight
        summed = jnp.dot(
            weights.astype(bf16),
            sv[:, :, piece].reshape(span, LANES),
            preferred_element_type=f32,
        )
        own_sums.append(
            summed + fresh_weight.astype(bf16).astype(f32) * fresh_values[k : k + 1]
        )
        own_peaks = jnp.where(own_lane == k, peak, own_peaks)
        own_totals = jnp.where(own_lane == k, total, own_totals)

    loop(1, n, lambda k: gather_one(STAT, ssend, srecv, k))
    head_lane = own_lane < KV_HEADS
    best = lax.fori_loop(0, n, lambda d, top: jnp.maximum(top, srecv[d]), own_peaks)
    own_factor = jnp.exp(own_peaks - best)
    loop(1, n, lambda k: gather_one(PART, psend, precv, k))

    def column(tile):
        return jnp.concatenate(
            [
                jnp.broadcast_to(tile[:, k : k + 1], (GROUP, LANES))
                for k in range(KV_HEADS)
            ],
            axis=0,
        )

    def merge(d, carry):
        numerator, denominator = carry
        stat = srecv[d]
        factor = jnp.where(head_lane, jnp.exp(jnp.minimum(stat - best, 0.0)), 0.0)
        denominator = denominator + factor * pltpu.roll(stat, LANES // 2, 1)
        return numerator + column(factor) * precv[d].astype(f32), denominator

    numerator, denominator = lax.fori_loop(
        0,
        n,
        merge,
        (column(own_factor) * jnp.concatenate(own_sums, axis=0), own_factor * own_totals),
    )
    denominator = jnp.where(head_lane, denominator, 1.0)
    attbuf[me] = (numerator / column(denominator)).astype(bf16)
    spread(ATT, attbuf)
    collect(ATT, attbuf)
    for j in range(HEADS // samples):
        rows = attbuf[:, j * samples : (j + 1) * samples, :].reshape(samples * samples, LANES)
        swapped = jnp.dot(square, rows, preferred_element_type=f32).astype(bf16)
        for i in range(samples):
            h = j * samples + i
            attl[
                h // per_device, :, (h % per_device) * LANES : (h % per_device + 1) * LANES
            ] = swapped[i * samples : (i + 1) * samples]

    def o_step(d, total):
        chunk(1, d).wait()
        return total + jnp.dot(attl[d], ow[rows_of(d), :], preferred_element_type=f32)

    attended = lax.fori_loop(0, n, o_step, jnp.zeros((samples, width), f32))
    mixbuf[me] = (tokbuf[me].astype(f32) + attended).astype(bf16)
    spread(MIX, mixbuf)
    collect(MIX, mixbuf)
    root = inverse_root(mixbuf)

    def ffn_step(d, carry):
        gate, up = carry
        chunk(2, d).wait()
        chunk(3, d).wait()
        part = normed(mixbuf, root, mgain, d)
        gate = gate + jnp.dot(part, gw[rows_of(d), :], preferred_element_type=f32)
        up = up + jnp.dot(part, uw[rows_of(d), :], preferred_element_type=f32)
        return gate, up

    zero = jnp.zeros((samples, ffn), f32)
    gate, up = lax.fori_loop(0, n, ffn_step, (zero, zero))
    hidden = (gate / (1.0 + jnp.exp(-gate)) * up).astype(bf16)

    def down_step(step, weights, place):
        down_chunk(step, weights, place).wait()
        term = jnp.dot(
            hidden,
            weights[pl.ds(pl.multiple_of(place * ffn, ffn), ffn), :],
            preferred_element_type=f32,
        )
        return term

    def down_low(i):
        dsend[(me + 1 + i) % n] = down_step(i, dw, i).astype(bf16)
        scatter_one(DOWN, dsend, drecv, i + 1)

    def down_high(i):
        dsend[(me + 1 + i) % n] = down_step(i, qw, i - half).astype(bf16)
        scatter_one(DOWN, dsend, drecv, i + 1)

    loop(0, half, down_low)
    loop(half, n - 1, down_high)
    total = mixbuf[me].astype(f32) + down_step(n - 1, qw, half - 1)

    for phase, buf in ((TOK, tokbuf), (QRY, qbuf), (ATT, attbuf), (MIX, mixbuf)):
        drain(phase, buf)
    for phase, source, target in (
        (FRESH, fsend, frecv),
        (STAT, ssend, srecv),
        (PART, psend, precv),
    ):
        loop(1, n, functools.partial(sent_one, phase, source, target))

    def finish(k, total):
        gather_one(DOWN, dsend, drecv, k)
        return total + drecv[(me + n - k) % n].astype(f32)

    total = lax.fori_loop(1, n, finish, total)
    out[...] = total.astype(bf16)
    loop(1, n, functools.partial(sent_one, DOWN, dsend, drecv))


def body(*args):
    tokens, q_weight, gate_weight = args[0], args[3], args[7]
    prefix_keys, suffix_keys, suffix_table = args[10], args[12], args[15]
    n = lax.axis_size("ctx")
    samples, width = tokens.shape
    ffn = gate_weight.shape[1]
    fits = (
        samples == n == FITS == 2 * KV_HEADS
        and suffix_table.shape[0] == 1
        and width % LANES == 0
        and n * width == HEADS * HEAD_DIM
        and q_weight.shape[0] == (n // 2) * ffn
        and suffix_keys.shape[0] * suffix_keys.shape[1] == LANES
    )
    if not fits:
        return plain_body(*args)
    args = list(args)
    args[1] = args[1].reshape(1, -1)
    args[2] = args[2].reshape(1, -1)
    bf16, f32 = jnp.bfloat16, jnp.float32
    kept = [args[i] for i in (3, 4, 5, 6, 7, 8)]
    exchange = pltpu.VMEM((n, samples, width), bf16)
    parts = pltpu.VMEM((n, HEADS, LANES), bf16)
    stats = pltpu.VMEM((n, GROUP, LANES), f32)
    fresh = pltpu.VMEM((n, 2 * KV_HEADS, LANES), f32)
    anywhere = pl.BlockSpec(memory_space=pl.ANY)
    scalars = pl.BlockSpec(memory_space=pltpu.SMEM)
    return pl.pallas_call(
        functools.partial(layer_kernel, n, prefix_keys.shape[0] * n),
        out_shape=jax.ShapeDtypeStruct((samples, width), bf16),
        in_specs=[anywhere] * 14 + [scalars] * 2,
        out_specs=pl.BlockSpec(memory_space=pltpu.VMEM),
        scratch_shapes=[pltpu.VMEM(w.shape, bf16) for w in kept]
        + [pltpu.VMEM(((n // 2) * ffn, width), bf16)]
        + [pltpu.VMEM(args[i].shape, bf16) for i in (10, 11, 12, 13)]
        + [pltpu.VMEM((1, n * width), f32)] * 2
        + [
            exchange,
            exchange,
            pltpu.VMEM((KV_HEADS, samples * GROUP, LANES), f32),
            parts,
            parts,
            stats,
            stats,
            fresh,
            fresh,
            parts,
            exchange,
            exchange,
            exchange,
            exchange,
            pltpu.SemaphoreType.DMA((9,)),
            pltpu.SemaphoreType.DMA((5, n)),
            pltpu.SemaphoreType.DMA((PHASES, n)),
            pltpu.SemaphoreType.DMA((PHASES, n)),
        ],
        compiler_params=pltpu.CompilerParams(
            collective_id=0, has_side_effects=True, vmem_limit_bytes=67043328
        ),
        name="layer",
    )(*args)


def solution(mesh):
    placed = (
        P("groups", "ctx"),
        P(),
        P(),
        P(None, "ctx"),
        P("ctx", None),
        P("ctx", None),
        P(None, "ctx"),
        P(None, "ctx"),
        P(None, "ctx"),
        P("ctx", None),
        P(("groups", "ctx"), None),
        P(("groups", "ctx"), None),
        P(("groups", "ctx"), None, None),
        P(("groups", "ctx"), None, None),
        P("groups"),
        P(("groups", "ctx"), None),
    )
    return jax.shard_map(
        body, mesh=mesh, in_specs=placed, out_specs=P("groups", "ctx"), check_vma=False
    )
```

```python
import functools
import math

import jax
import jax.numpy as jnp
from jax import lax
from jax.experimental import pallas as pl
from jax.experimental.pallas import tpu as pltpu
from jax.sharding import PartitionSpec as P

HEADS = 64
KV_HEADS = 8
HEAD_DIM = 128


EPSILON = 1e-05
ROPE_BASE = 500000.0


def rotate(matrix, position, columns):
    pair_index = (columns % HEAD_DIM // 2).astype(jnp.float32)
    frequency = jnp.exp(pair_index * (-2.0 * math.log(ROPE_BASE) / HEAD_DIM))
    angles = position.astype(jnp.float32)[:, None] * frequency[None, :]
    cosine = jnp.cos(angles[:, 0::2])
    sine_part = jnp.sin(angles[:, 0::2])
    even_part = matrix[:, 0::2]
    odd_part = matrix[:, 1::2]
    rotated_even = even_part * cosine - odd_part * sine_part
    rotated_odd = even_part * sine_part + odd_part * cosine
    return jnp.stack([rotated_even, rotated_odd], axis=-1).reshape(matrix.shape)


def normalized_rows(shard_rows, gain_vector):
    self_index = lax.axis_index("ctx")
    feature_width = shard_rows.shape[1]
    gathered_raw = lax.all_gather(shard_rows, "ctx", axis=1, tiled=True)
    widened = gathered_raw.astype(jnp.float32)
    mean_square = jnp.mean(widened * widened, axis=1, keepdims=True)
    gathered = (widened * lax.rsqrt(mean_square + EPSILON) * gain_vector).astype(jnp.bfloat16)
    local_part = lax.dynamic_slice_in_dim(gathered, self_index * feature_width, feature_width, 1)
    return (gathered, local_part)


def plain_body(
    tokens,
    attn_gain,
    mlp_gain,
    q_weight,
    k_weight,
    v_weight,
    o_weight,
    gate_weight,
    up_weight,
    down_weight,
    prefix_keys,
    prefix_values,
    suffix_keys,
    suffix_values,
    suffix_lengths,
    suffix_table,
):
    self_index = lax.axis_index("ctx")
    devices = lax.axis_size("ctx")
    samples = tokens.shape[0]
    own_rows = suffix_table.shape[0]
    group_size = HEADS // KV_HEADS
    score_scale = 1.0 / math.sqrt(HEAD_DIM)
    prefix_rows = prefix_keys.shape[0]
    row_start = self_index * own_rows
    position = prefix_rows * devices + suffix_lengths
    own_position = lax.dynamic_slice_in_dim(position, row_start, own_rows, 0)
    own_lengths = lax.dynamic_slice_in_dim(suffix_lengths, row_start, own_rows, 0)
    attn_normed, local_normed = normalized_rows(tokens, attn_gain)
    query_width = q_weight.shape[1]
    query_cols = self_index * query_width + jnp.arange(query_width, dtype=jnp.int32)
    query_part = rotate(
        jnp.dot(attn_normed, q_weight, preferred_element_type=jnp.float32), position, query_cols
    ).astype(jnp.bfloat16)
    queries = lax.all_gather(query_part, "ctx", axis=1, tiled=True)
    key_width = k_weight.shape[1]
    key_term = jnp.dot(local_normed, k_weight, preferred_element_type=jnp.float32)
    value_term = jnp.dot(local_normed, v_weight, preferred_element_type=jnp.float32)
    fresh = lax.psum_scatter(
        jnp.concatenate([key_term, value_term], axis=1), "ctx", scatter_dimension=0, tiled=True
    )
    fresh_keys = rotate(
        fresh[:, :key_width], own_position, jnp.arange(key_width, dtype=jnp.int32)
    ).astype(jnp.bfloat16)
    fresh_values = fresh[:, key_width:].astype(jnp.bfloat16)
    query_heads = queries.reshape(samples, KV_HEADS, group_size, HEAD_DIM)
    head_keys = prefix_keys.reshape(prefix_rows, KV_HEADS, HEAD_DIM)
    head_values = prefix_values.reshape(prefix_rows, KV_HEADS, HEAD_DIM)
    scores = (
        jnp.einsum("sngd,tnd->sngt", query_heads, head_keys, preferred_element_type=jnp.float32)
        * score_scale
    )
    local_peak = jnp.max(scores, axis=-1)
    peak_heads = lax.pmax(local_peak, "ctx")
    weights = jnp.exp(scores - peak_heads[..., None])
    partial_total = jnp.sum(weights, axis=-1).reshape(samples, HEADS)
    summed = jnp.einsum(
        "sngt,tnd->sngd",
        weights.astype(jnp.bfloat16),
        head_values,
        preferred_element_type=jnp.float32,
    ).reshape(samples, HEADS * HEAD_DIM)
    every_sum, every_total = lax.psum((summed, partial_total), "ctx")
    prefix_sum = lax.dynamic_slice_in_dim(every_sum, row_start, own_rows, 0)
    prefix_total = lax.dynamic_slice_in_dim(every_total, row_start, own_rows, 0)
    prefix_peak = lax.dynamic_slice_in_dim(
        peak_heads.reshape(samples, HEADS), row_start, own_rows, 0
    )
    prefix_sum = prefix_sum.reshape(own_rows, HEADS, HEAD_DIM)
    own_queries = lax.dynamic_slice_in_dim(query_heads, row_start, own_rows, 0)
    suffix_span = suffix_table.shape[1] * suffix_keys.shape[1]
    owned_keys = suffix_keys[suffix_table].reshape(own_rows, suffix_span, KV_HEADS, HEAD_DIM)
    owned_values = suffix_values[suffix_table].reshape(own_rows, suffix_span, KV_HEADS, HEAD_DIM)
    every_key = jnp.concatenate(
        [owned_keys, fresh_keys.reshape(own_rows, 1, KV_HEADS, HEAD_DIM)], axis=1
    )
    every_value = jnp.concatenate(
        [owned_values, fresh_values.reshape(own_rows, 1, KV_HEADS, HEAD_DIM)], axis=1
    )
    slot_index = jnp.arange(suffix_span + 1, dtype=jnp.int32)
    live_mask = (slot_index[None, :] < own_lengths[:, None]) | (slot_index[None, :] == suffix_span)
    suffix_scores = (
        jnp.einsum("sngd,sjnd->sngj", own_queries, every_key, preferred_element_type=jnp.float32)
        * score_scale
    )
    suffix_scores = jnp.where(live_mask[:, None, None, :], suffix_scores, -1e30)
    suffix_peak = jnp.max(suffix_scores, axis=-1)
    suffix_weights = jnp.exp(suffix_scores - suffix_peak[..., None])
    suffix_total = jnp.sum(suffix_weights, axis=-1).reshape(own_rows, HEADS)
    suffix_sum = jnp.einsum(
        "sngj,sjnd->sngd",
        suffix_weights.astype(jnp.bfloat16),
        every_value,
        preferred_element_type=jnp.float32,
    ).reshape(own_rows, HEADS, HEAD_DIM)
    suffix_peak = suffix_peak.reshape(own_rows, HEADS)
    peak_all = jnp.maximum(prefix_peak, suffix_peak)
    prefix_factor = jnp.exp(prefix_peak - peak_all)
    suffix_factor = jnp.exp(suffix_peak - peak_all)
    numerator = prefix_sum * prefix_factor[..., None] + suffix_sum * suffix_factor[..., None]
    denominator = prefix_total * prefix_factor + suffix_total * suffix_factor
    attention = (
        (numerator / denominator[..., None])
        .reshape(own_rows, HEADS * HEAD_DIM)
        .astype(jnp.bfloat16)
    )
    attended = jnp.dot(
        lax.all_gather(attention, "ctx", axis=0, tiled=True),
        o_weight,
        preferred_element_type=jnp.float32,
    )
    mixed_rows = (tokens.astype(jnp.float32) + attended).astype(jnp.bfloat16)
    mlp_normed = normalized_rows(mixed_rows, mlp_gain)[0]
    gate_proj = jnp.dot(mlp_normed, gate_weight, preferred_element_type=jnp.float32)
    up_proj = jnp.dot(mlp_normed, up_weight, preferred_element_type=jnp.float32)
    hidden = (jax.nn.silu(gate_proj) * up_proj).astype(jnp.bfloat16)
    partial_value = jnp.dot(hidden, down_weight, preferred_element_type=jnp.float32)
    shares = lax.psum_scatter(partial_value, "ctx", scatter_dimension=1, tiled=True)
    return (mixed_rows.astype(jnp.float32) + shares).astype(jnp.bfloat16)


TOK, QRY, FRESH, PART, STAT, ATT, MIX, PAIR, DOWN, PHASES = range(10)
LANES = HEAD_DIM
GROUP = HEADS // KV_HEADS
FITS = 16


def regroup(rows, inner, outer):
    row = lax.broadcasted_iota(jnp.int32, (rows, rows), 0)
    column = lax.broadcasted_iota(jnp.int32, (rows, rows), 1)
    picked = (row % outer) * inner + row // outer
    return jnp.where(column == picked, 1.0, 0.0).astype(jnp.bfloat16)


def turn(block, cosine, signed_sine, even):
    swapped = jnp.where(even, pltpu.roll(block, LANES - 1, 1), pltpu.roll(block, 1, 1))
    return block * cosine + swapped * signed_sine


def layer_kernel(
    n,
    prefix_tokens,
    tokens,
    attn_gain,
    mlp_gain,
    q_hbm,
    k_hbm,
    v_hbm,
    o_hbm,
    gate_hbm,
    up_hbm,
    down_hbm,
    pk_hbm,
    pv_hbm,
    sk_hbm,
    sv_hbm,
    lengths,
    table,
    out,
    qw,
    kw,
    vw,
    ow,
    gw,
    uw,
    dw,
    pk,
    pv,
    sk,
    sv,
    again,
    mgain,
    tokbuf,
    qbuf,
    qperm,
    psend,
    precv,
    ssend,
    srecv,
    fsend,
    frecv,
    attbuf,
    mixbuf,
    dsend,
    dpair,
    drecv,
    load_sem,
    big_sem,
    send_sem,
    recv_sem,
):
    me = lax.axis_index("ctx")
    partner = me + 1 - 2 * (me % 2)
    half = n // 2
    core = me % 2
    chip = me // 2
    samples, width = tokens.shape
    ffn = gw.shape[1]
    scale = 1.0 / math.sqrt(HEAD_DIM)
    f32, bf16 = jnp.float32, jnp.bfloat16

    def load(source, target, index):
        return pltpu.make_async_copy(source, target, load_sem.at[index])

    def rows_of(d):
        return pl.ds(pl.multiple_of(d * width, width), width)

    def chunk(kind, d):
        if kind == 0:
            return pltpu.make_async_copy(q_hbm.at[rows_of(d)], qw.at[rows_of(d)], big_sem.at[0, d])
        if kind == 1:
            return pltpu.make_async_copy(o_hbm.at[rows_of(d)], ow.at[rows_of(d)], big_sem.at[1, d])
        if kind == 2:
            return pltpu.make_async_copy(
                gate_hbm.at[rows_of(d)], gw.at[rows_of(d)], big_sem.at[2, d]
            )
        return pltpu.make_async_copy(up_hbm.at[rows_of(d)], uw.at[rows_of(d)], big_sem.at[3, d])

    def down_chunk(step, target, place):
        d = 2 * ((chip + 1 + step) % half) + (core + 1 + step // half) % 2
        return pltpu.make_async_copy(
            down_hbm.at[:, rows_of(d)],
            target.at[pl.ds(pl.multiple_of(place * ffn, ffn), ffn)],
            big_sem.at[4, step],
        )

    def remote(phase, source, target, slot, landed, device):
        return pltpu.make_async_remote_copy(
            src_ref=source,
            dst_ref=target,
            send_sem=send_sem.at[phase, slot],
            recv_sem=recv_sem.at[phase, landed],
            device_id={"ctx": device},
            device_id_type=pl.DeviceIdType.MESH,
        )

    def loop(low, high, step):
        def wrapped(index, carry):
            step(index)
            return carry

        lax.fori_loop(low, high, wrapped, 0)

    def spread(phase, buf):
        loop(
            1,
            half,
            lambda k: remote(
                phase, buf.at[me], buf.at[me], k, me, (me + 2 * k) % n
            ).start(),
        )
        remote(phase, buf.at[me], buf.at[me], 0, me, partner).start()

    def collect(phase, buf):
        def relay(k):
            origin = (me + n - 2 * k) % n
            remote(phase, buf.at[origin], buf.at[origin], 0, origin, partner).wait_recv()
            remote(phase, buf.at[origin], buf.at[origin], half + k, origin, partner).start()

        def arrive(k):
            origin = (partner + n - 2 * k) % n
            remote(phase, buf.at[origin], buf.at[origin], 0, origin, partner).wait_recv()

        loop(1, half, relay)
        loop(0, half, arrive)

    def drain(phase, buf):
        def one(k):
            remote(phase, buf.at[me], buf.at[me], k, me, partner).wait_send()

        loop(0, half, one)
        loop(half + 1, n, one)

    def scatter_one(phase, source, target, k):
        device = (me + k) % n
        remote(phase, source.at[device], target.at[me], k, me, device).start()

    def gather_one(phase, source, target, k):
        origin = (me + n - k) % n
        remote(phase, source.at[origin], target.at[origin], k, origin, origin).wait_recv()

    def sent_one(phase, source, target, k):
        device = (me + k) % n
        remote(phase, source.at[device], target.at[me], k, me, device).wait_send()

    first = load(tokens, tokbuf.at[me], 0)
    first.start()
    small = [
        load(attn_gain, again, 1),
        load(mlp_gain, mgain, 2),
        load(k_hbm, kw, 3),
        load(v_hbm, vw, 4),
        load(pk_hbm, pk, 5),
        load(pv_hbm, pv, 6),
        load(sk_hbm, sk, 7),
        load(sv_hbm, sv, 8),
    ]
    barrier = pltpu.get_barrier_semaphore()
    loop(
        1,
        n,
        lambda k: pl.semaphore_signal(
            barrier,
            inc=1,
            device_id={"ctx": (me + k) % n},
            device_id_type=pl.DeviceIdType.MESH,
        ),
    )
    small[0].start()
    loop(0, n, lambda d: chunk(0, d).start())
    for copy in small[1:]:
        copy.start()
    first.wait()
    pl.semaphore_wait(barrier, n - 1)
    spread(TOK, tokbuf)
    loop(0, n, lambda d: chunk(1, d).start())

    def start_pair(d):
        chunk(2, d).start()
        chunk(3, d).start()

    loop(0, n, start_pair)
    loop(0, half, lambda i: down_chunk(i, dw, i).start())

    lane = lax.broadcasted_iota(jnp.int32, (samples, LANES), 1)
    row = lax.broadcasted_iota(jnp.int32, (samples, LANES), 0)
    even = lane % 2 == 0
    pair_index = (lane // 2).astype(f32)
    frequency = jnp.exp(pair_index * (-2.0 * math.log(ROPE_BASE) / HEAD_DIM))
    position = jnp.zeros((samples, LANES), jnp.int32)
    for s in range(samples):
        position = jnp.where(row == s, lengths[s] + prefix_tokens, position)
    angles = position.astype(f32) * frequency
    cosine = jnp.cos(angles)
    sine = jnp.where(even, -1.0, 1.0) * jnp.sin(angles)
    own_length = lengths[me]
    own_angles = (own_length + prefix_tokens).astype(f32) * frequency
    own_cosine = jnp.cos(own_angles)[:KV_HEADS]
    own_sine = (jnp.where(even, -1.0, 1.0) * jnp.sin(own_angles))[:KV_HEADS]
    to_sample = regroup(samples * GROUP, samples, GROUP)
    square = regroup(samples * samples, samples, samples)

    def inverse_root(buf):
        def add(d, total):
            block = buf[d].astype(f32)
            return total + jnp.sum(block * block, axis=1, keepdims=True)

        total = lax.fori_loop(0, n, add, jnp.zeros((samples, 1), f32), unroll=True)
        return lax.rsqrt(total / (n * width) + EPSILON)

    def normed(buf, root, gain, d):
        return (buf[d].astype(f32) * root * gain[:, rows_of(d)]).astype(bf16)

    for copy in small[:2]:
        copy.wait()
    collect(TOK, tokbuf)
    root = inverse_root(tokbuf)

    def q_step(d, total):
        chunk(0, d).wait()
        return total + jnp.dot(
            normed(tokbuf, root, again, d), qw[rows_of(d), :], preferred_element_type=f32
        )

    query = lax.fori_loop(0, n, q_step, jnp.zeros((samples, width), f32), unroll=4)
    for j in range(width // LANES):
        piece = slice(j * LANES, (j + 1) * LANES)
        qbuf[me, :, piece] = turn(query[:, piece], cosine, sine, even).astype(bf16)
    spread(QRY, qbuf)
    loop(half, n, lambda i: down_chunk(i, qw, i - half).start())

    for copy in small[2:]:
        copy.wait()
    mine = normed(tokbuf, root, again, me)
    terms = [
        jnp.dot(mine, kw[...], preferred_element_type=f32),
        jnp.dot(mine, vw[...], preferred_element_type=f32),
    ]
    stacked = jnp.concatenate(
        [
            term[:, c * LANES : (c + 1) * LANES]
            for term in terms
            for c in range(KV_HEADS)
        ],
        axis=0,
    )
    upper = stacked.astype(bf16)
    lower = (stacked - upper.astype(f32)).astype(bf16)
    by_owner = jnp.dot(square, upper, preferred_element_type=f32) + jnp.dot(
        square, lower, preferred_element_type=f32
    )
    by_owner = by_owner.reshape(n, 2 * KV_HEADS, LANES)
    fsend[...] = by_owner
    collect(QRY, qbuf)
    loop(1, n, lambda k: scatter_one(FRESH, fsend, frecv, k))
    frecv[me] = fsend[me]
    stat_lane = lax.broadcasted_iota(jnp.int32, (samples * GROUP, LANES), 1)
    stats = jnp.zeros((samples * GROUP, LANES), f32)
    per_device = width // LANES
    held = []
    for k in range(KV_HEADS):
        piece = slice(k * LANES, (k + 1) * LANES)
        heads = [k * GROUP + g for g in range(GROUP)]
        raw = jnp.concatenate(
            [
                qbuf[h // per_device, :, (h % per_device) * LANES : (h % per_device + 1) * LANES]
                for h in heads
            ],
            axis=0,
        )
        arranged = jnp.dot(to_sample, raw, preferred_element_type=f32)
        qperm[k] = arranged.astype(bf16).reshape(samples, GROUP, LANES)
        scores = (
            lax.dot_general(
                arranged.astype(bf16),
                pk[:, piece],
                (((1,), (1,)), ((), ())),
                preferred_element_type=f32,
            )
            * scale
        )
        peak = jnp.max(scores, axis=1, keepdims=True)
        weights = jnp.exp(scores - peak)
        total = jnp.sum(weights, axis=1, keepdims=True)
        summed = jnp.dot(weights.astype(bf16), pv[:, piece], preferred_element_type=f32)
        stats = jnp.where(stat_lane == k, peak, stats)
        stats = jnp.where(stat_lane == k + LANES // 2, total, stats)
        held.append(summed.reshape(samples, GROUP, LANES))
        if k % 2 == 1:
            psend[:, (k - 1) * GROUP : (k + 1) * GROUP, :] = jnp.concatenate(
                held, axis=1
            ).astype(bf16)
            held = []
    ssend[...] = stats.reshape(samples, GROUP, LANES)

    def send_part(k):
        scatter_one(STAT, ssend, srecv, k)
        scatter_one(PART, psend, precv, k)

    loop(1, n, send_part)
    srecv[me] = ssend[me]
    precv[me] = psend[me]

    loop(1, n, lambda k: gather_one(FRESH, fsend, frecv, k))
    fresh = lax.fori_loop(
        0, n, lambda d, total: total + frecv[d], jnp.zeros((2 * KV_HEADS, LANES), f32), unroll=True
    )
    fresh_keys = (
        turn(fresh[:KV_HEADS], own_cosine, own_sine, even[:KV_HEADS]).astype(bf16).astype(f32)
    )
    fresh_values = fresh[KV_HEADS:].astype(bf16).astype(f32)
    blocks, block = sk.shape[0], sk.shape[1]
    span = blocks * block
    place = lax.broadcasted_iota(jnp.int32, (GROUP, span), 1)
    slot = jnp.zeros((GROUP, span), jnp.int32)
    for i in range(blocks):
        slot = jnp.where(place // block == table[0, i], i * block + place % block, slot)
    live = slot < own_length
    own_lane = lax.broadcasted_iota(jnp.int32, (GROUP, LANES), 1)
    own_peaks = jnp.zeros((GROUP, LANES), f32)
    own_totals = jnp.zeros((GROUP, LANES), f32)
    own_sums = []
    for k in range(KV_HEADS):
        piece = slice(k * LANES, (k + 1) * LANES)
        mine_q = qperm[k, me].astype(f32)
        scores = (
            lax.dot_general(
                mine_q.astype(bf16),
                sk[:, :, piece].reshape(span, LANES),
                (((1,), (1,)), ((), ())),
                preferred_element_type=f32,
            )
            * scale
        )
        scores = jnp.where(live, scores, -1e30)
        fresh_score = (
            jnp.sum(mine_q * fresh_keys[k : k + 1], axis=1, keepdims=True) * scale
        )
        peak = jnp.maximum(jnp.max(scores, axis=1, keepdims=True), fresh_score)
        weights = jnp.where(live, jnp.exp(scores - peak), 0.0)
        fresh_weight = jnp.exp(fresh_score - peak)
        total = jnp.sum(weights, axis=1, keepdims=True) + fresh_weight
        summed = jnp.dot(
            weights.astype(bf16),
            sv[:, :, piece].reshape(span, LANES),
            preferred_element_type=f32,
        )
        own_sums.append(
            summed + fresh_weight.astype(bf16).astype(f32) * fresh_values[k : k + 1]
        )
        own_peaks = jnp.where(own_lane == k, peak, own_peaks)
        own_totals = jnp.where(own_lane == k, total, own_totals)

    loop(1, n, lambda k: gather_one(STAT, ssend, srecv, k))
    head_lane = own_lane < KV_HEADS
    best = lax.fori_loop(0, n, lambda d, top: jnp.maximum(top, srecv[d]), own_peaks, unroll=True)
    own_factor = jnp.exp(own_peaks - best)
    loop(1, n, lambda k: gather_one(PART, psend, precv, k))

    def column(tile):
        return jnp.concatenate(
            [
                jnp.broadcast_to(tile[:, k : k + 1], (GROUP, LANES))
                for k in range(KV_HEADS)
            ],
            axis=0,
        )

    def merge(d, carry):
        numerator, denominator = carry
        stat = srecv[d]
        factor = jnp.where(head_lane, jnp.exp(jnp.minimum(stat - best, 0.0)), 0.0)
        denominator = denominator + factor * pltpu.roll(stat, LANES // 2, 1)
        return numerator + column(factor) * precv[d].astype(f32), denominator

    numerator, denominator = lax.fori_loop(
        0,
        n,
        merge,
        (column(own_factor) * jnp.concatenate(own_sums, axis=0), own_factor * own_totals),
        unroll=2,
    )
    denominator = jnp.where(head_lane, denominator, 1.0)
    attbuf[me] = (numerator / column(denominator)).astype(bf16)
    spread(ATT, attbuf)
    drain(QRY, qbuf)
    collect(ATT, attbuf)
    for j in range(HEADS // samples):
        rows = attbuf[:, j * samples : (j + 1) * samples, :].reshape(samples * samples, LANES)
        swapped = jnp.dot(square, rows, preferred_element_type=f32).astype(bf16)
        for i in range(samples):
            h = j * samples + i
            qbuf[
                h // per_device, :, (h % per_device) * LANES : (h % per_device + 1) * LANES
            ] = swapped[i * samples : (i + 1) * samples]

    def o_step(d, total):
        chunk(1, d).wait()
        return total + jnp.dot(qbuf[d], ow[rows_of(d), :], preferred_element_type=f32)

    attended = lax.fori_loop(0, n, o_step, jnp.zeros((samples, width), f32), unroll=4)
    mixbuf[me] = (tokbuf[me].astype(f32) + attended).astype(bf16)
    spread(MIX, mixbuf)
    collect(MIX, mixbuf)
    root = inverse_root(mixbuf)

    def ffn_step(d, carry):
        gate, up = carry
        chunk(2, d).wait()
        chunk(3, d).wait()
        part = normed(mixbuf, root, mgain, d)
        gate = gate + jnp.dot(part, gw[rows_of(d), :], preferred_element_type=f32)
        up = up + jnp.dot(part, uw[rows_of(d), :], preferred_element_type=f32)
        return gate, up

    zero = jnp.zeros((samples, ffn), f32)
    gate, up = lax.fori_loop(0, n, ffn_step, (zero, zero), unroll=4)
    hidden = (gate / (1.0 + jnp.exp(-gate)) * up).astype(bf16)

    def down_step(step, weights, place):
        down_chunk(step, weights, place).wait()
        term = jnp.dot(
            hidden,
            weights[pl.ds(pl.multiple_of(place * ffn, ffn), ffn), :],
            preferred_element_type=f32,
        )
        return term

    def to_pair(c, slot):
        return remote(PAIR, dsend.at[c], dpair.at[c], slot, c, partner)

    def down_low(i, carry):
        c = (chip + 1 + i) % half
        dsend[c] = down_step(i, dw, i).astype(bf16)
        to_pair(c, i).start()
        return carry

    lax.fori_loop(0, half, down_low, 0, unroll=2)

    def to_chip(k):
        c = (chip + k) % half
        return remote(DOWN, dpair.at[c], drecv.at[chip], k, chip, 2 * c + core)

    def down_high(i, carry):
        c = (chip + 1 + i) % half
        term = down_step(half + i, qw, i)
        to_pair(c, 0).wait_recv()
        dpair[c] = (term + dpair[c].astype(f32)).astype(bf16)
        to_chip(i + 1).start()
        return carry

    lax.fori_loop(0, half - 1, down_high, 0)
    total = mixbuf[me].astype(f32) + down_step(n - 1, qw, half - 1)
    to_pair(chip, 0).wait_recv()
    total = total + dpair[chip].astype(f32)

    for phase, buf in ((TOK, tokbuf), (ATT, attbuf), (MIX, mixbuf)):
        drain(phase, buf)
    for phase, source, target in (
        (FRESH, fsend, frecv),
        (STAT, ssend, srecv),
        (PART, psend, precv),
    ):
        loop(1, n, functools.partial(sent_one, phase, source, target))

    def finish(k, total):
        origin = (chip + half - k) % half
        remote(
            DOWN, dpair.at[origin], drecv.at[origin], 0, origin, 2 * origin + core
        ).wait_recv()
        return total + drecv[origin].astype(f32)

    total = lax.fori_loop(1, half, finish, total)
    out[...] = total.astype(bf16)
    loop(0, half, lambda i: to_pair((chip + 1 + i) % half, i).wait_send())
    loop(1, half, lambda k: to_chip(k).wait_send())


def body(*args):
    tokens, q_weight, gate_weight = args[0], args[3], args[7]
    prefix_keys, suffix_keys, suffix_table = args[10], args[12], args[15]
    n = lax.axis_size("ctx")
    samples, width = tokens.shape
    ffn = gate_weight.shape[1]
    fits = (
        samples == n == FITS == 2 * KV_HEADS
        and suffix_table.shape[0] == 1
        and width % LANES == 0
        and n * width == HEADS * HEAD_DIM
        and q_weight.shape[0] == (n // 2) * ffn
        and suffix_keys.shape[0] * suffix_keys.shape[1] == LANES
    )
    if not fits:
        return plain_body(*args)
    args = list(args)
    args[1] = args[1].reshape(1, -1)
    args[2] = args[2].reshape(1, -1)
    bf16, f32 = jnp.bfloat16, jnp.float32
    kept = [args[i] for i in (3, 4, 5, 6, 7, 8)]
    exchange = pltpu.VMEM((n, samples, width), bf16)
    parts = pltpu.VMEM((n, HEADS, LANES), bf16)
    stats = pltpu.VMEM((n, GROUP, LANES), f32)
    fresh = pltpu.VMEM((n, 2 * KV_HEADS, LANES), f32)
    anywhere = pl.BlockSpec(memory_space=pl.ANY)
    scalars = pl.BlockSpec(memory_space=pltpu.SMEM)
    return pl.pallas_call(
        functools.partial(layer_kernel, n, prefix_keys.shape[0] * n),
        out_shape=jax.ShapeDtypeStruct((samples, width), bf16),
        in_specs=[anywhere] * 14 + [scalars] * 2,
        out_specs=pl.BlockSpec(memory_space=pltpu.VMEM),
        scratch_shapes=[pltpu.VMEM(w.shape, bf16) for w in kept]
        + [pltpu.VMEM(((n // 2) * ffn, width), bf16)]
        + [pltpu.VMEM(args[i].shape, bf16) for i in (10, 11, 12, 13)]
        + [pltpu.VMEM((1, n * width), f32)] * 2
        + [
            exchange,
            exchange,
            pltpu.VMEM((KV_HEADS, samples, GROUP, LANES), bf16),
            parts,
            parts,
            stats,
            stats,
            fresh,
            fresh,
            parts,
            exchange,
            pltpu.VMEM((n // 2, samples, width), bf16),
            pltpu.VMEM((n // 2, samples, width), bf16),
            pltpu.VMEM((n // 2, samples, width), bf16),
            pltpu.SemaphoreType.DMA((9,)),
            pltpu.SemaphoreType.DMA((5, n)),
            pltpu.SemaphoreType.DMA((PHASES, n)),
            pltpu.SemaphoreType.DMA((PHASES, n)),
        ],
        compiler_params=pltpu.CompilerParams(
            collective_id=0, has_side_effects=True, vmem_limit_bytes=67043328
        ),
        name="layer",
    )(*args)


def solution(mesh):
    placed = (
        P("groups", "ctx"),
        P(),
        P(),
        P(None, "ctx"),
        P("ctx", None),
        P("ctx", None),
        P(None, "ctx"),
        P(None, "ctx"),
        P(None, "ctx"),
        P("ctx", None),
        P(("groups", "ctx"), None),
        P(("groups", "ctx"), None),
        P(("groups", "ctx"), None, None),
        P(("groups", "ctx"), None, None),
        P("groups"),
        P(("groups", "ctx"), None),
    )
    return jax.shard_map(
        body, mesh=mesh, in_specs=placed, out_specs=P("groups", "ctx"), check_vma=False
    )
```

```python
import functools
import math

import jax
import jax.numpy as jnp
from jax import lax
from jax.experimental import pallas as pl
from jax.experimental.pallas import tpu as pltpu
from jax.sharding import PartitionSpec as P

HEADS = 64
KV_HEADS = 8
HEAD_DIM = 128


EPSILON = 1e-05
ROPE_BASE = 500000.0


def rotate(matrix, position, columns):
    pair_index = (columns % HEAD_DIM // 2).astype(jnp.float32)
    frequency = jnp.exp(pair_index * (-2.0 * math.log(ROPE_BASE) / HEAD_DIM))
    angles = position.astype(jnp.float32)[:, None] * frequency[None, :]
    cosine = jnp.cos(angles[:, 0::2])
    sine_part = jnp.sin(angles[:, 0::2])
    even_part = matrix[:, 0::2]
    odd_part = matrix[:, 1::2]
    rotated_even = even_part * cosine - odd_part * sine_part
    rotated_odd = even_part * sine_part + odd_part * cosine
    return jnp.stack([rotated_even, rotated_odd], axis=-1).reshape(matrix.shape)


def normalized_rows(shard_rows, gain_vector):
    self_index = lax.axis_index("ctx")
    feature_width = shard_rows.shape[1]
    gathered_raw = lax.all_gather(shard_rows, "ctx", axis=1, tiled=True)
    widened = gathered_raw.astype(jnp.float32)
    mean_square = jnp.mean(widened * widened, axis=1, keepdims=True)
    gathered = (widened * lax.rsqrt(mean_square + EPSILON) * gain_vector).astype(jnp.bfloat16)
    local_part = lax.dynamic_slice_in_dim(gathered, self_index * feature_width, feature_width, 1)
    return (gathered, local_part)


def plain_body(
    tokens,
    attn_gain,
    mlp_gain,
    q_weight,
    k_weight,
    v_weight,
    o_weight,
    gate_weight,
    up_weight,
    down_weight,
    prefix_keys,
    prefix_values,
    suffix_keys,
    suffix_values,
    suffix_lengths,
    suffix_table,
):
    self_index = lax.axis_index("ctx")
    devices = lax.axis_size("ctx")
    samples = tokens.shape[0]
    own_rows = suffix_table.shape[0]
    group_size = HEADS // KV_HEADS
    score_scale = 1.0 / math.sqrt(HEAD_DIM)
    prefix_rows = prefix_keys.shape[0]
    row_start = self_index * own_rows
    position = prefix_rows * devices + suffix_lengths
    own_position = lax.dynamic_slice_in_dim(position, row_start, own_rows, 0)
    own_lengths = lax.dynamic_slice_in_dim(suffix_lengths, row_start, own_rows, 0)
    attn_normed, local_normed = normalized_rows(tokens, attn_gain)
    query_width = q_weight.shape[1]
    query_cols = self_index * query_width + jnp.arange(query_width, dtype=jnp.int32)
    query_part = rotate(
        jnp.dot(attn_normed, q_weight, preferred_element_type=jnp.float32), position, query_cols
    ).astype(jnp.bfloat16)
    queries = lax.all_gather(query_part, "ctx", axis=1, tiled=True)
    key_width = k_weight.shape[1]
    key_term = jnp.dot(local_normed, k_weight, preferred_element_type=jnp.float32)
    value_term = jnp.dot(local_normed, v_weight, preferred_element_type=jnp.float32)
    fresh = lax.psum_scatter(
        jnp.concatenate([key_term, value_term], axis=1), "ctx", scatter_dimension=0, tiled=True
    )
    fresh_keys = rotate(
        fresh[:, :key_width], own_position, jnp.arange(key_width, dtype=jnp.int32)
    ).astype(jnp.bfloat16)
    fresh_values = fresh[:, key_width:].astype(jnp.bfloat16)
    query_heads = queries.reshape(samples, KV_HEADS, group_size, HEAD_DIM)
    head_keys = prefix_keys.reshape(prefix_rows, KV_HEADS, HEAD_DIM)
    head_values = prefix_values.reshape(prefix_rows, KV_HEADS, HEAD_DIM)
    scores = (
        jnp.einsum("sngd,tnd->sngt", query_heads, head_keys, preferred_element_type=jnp.float32)
        * score_scale
    )
    local_peak = jnp.max(scores, axis=-1)
    peak_heads = lax.pmax(local_peak, "ctx")
    weights = jnp.exp(scores - peak_heads[..., None])
    partial_total = jnp.sum(weights, axis=-1).reshape(samples, HEADS)
    summed = jnp.einsum(
        "sngt,tnd->sngd",
        weights.astype(jnp.bfloat16),
        head_values,
        preferred_element_type=jnp.float32,
    ).reshape(samples, HEADS * HEAD_DIM)
    every_sum, every_total = lax.psum((summed, partial_total), "ctx")
    prefix_sum = lax.dynamic_slice_in_dim(every_sum, row_start, own_rows, 0)
    prefix_total = lax.dynamic_slice_in_dim(every_total, row_start, own_rows, 0)
    prefix_peak = lax.dynamic_slice_in_dim(
        peak_heads.reshape(samples, HEADS), row_start, own_rows, 0
    )
    prefix_sum = prefix_sum.reshape(own_rows, HEADS, HEAD_DIM)
    own_queries = lax.dynamic_slice_in_dim(query_heads, row_start, own_rows, 0)
    suffix_span = suffix_table.shape[1] * suffix_keys.shape[1]
    owned_keys = suffix_keys[suffix_table].reshape(own_rows, suffix_span, KV_HEADS, HEAD_DIM)
    owned_values = suffix_values[suffix_table].reshape(own_rows, suffix_span, KV_HEADS, HEAD_DIM)
    every_key = jnp.concatenate(
        [owned_keys, fresh_keys.reshape(own_rows, 1, KV_HEADS, HEAD_DIM)], axis=1
    )
    every_value = jnp.concatenate(
        [owned_values, fresh_values.reshape(own_rows, 1, KV_HEADS, HEAD_DIM)], axis=1
    )
    slot_index = jnp.arange(suffix_span + 1, dtype=jnp.int32)
    live_mask = (slot_index[None, :] < own_lengths[:, None]) | (slot_index[None, :] == suffix_span)
    suffix_scores = (
        jnp.einsum("sngd,sjnd->sngj", own_queries, every_key, preferred_element_type=jnp.float32)
        * score_scale
    )
    suffix_scores = jnp.where(live_mask[:, None, None, :], suffix_scores, -1e30)
    suffix_peak = jnp.max(suffix_scores, axis=-1)
    suffix_weights = jnp.exp(suffix_scores - suffix_peak[..., None])
    suffix_total = jnp.sum(suffix_weights, axis=-1).reshape(own_rows, HEADS)
    suffix_sum = jnp.einsum(
        "sngj,sjnd->sngd",
        suffix_weights.astype(jnp.bfloat16),
        every_value,
        preferred_element_type=jnp.float32,
    ).reshape(own_rows, HEADS, HEAD_DIM)
    suffix_peak = suffix_peak.reshape(own_rows, HEADS)
    peak_all = jnp.maximum(prefix_peak, suffix_peak)
    prefix_factor = jnp.exp(prefix_peak - peak_all)
    suffix_factor = jnp.exp(suffix_peak - peak_all)
    numerator = prefix_sum * prefix_factor[..., None] + suffix_sum * suffix_factor[..., None]
    denominator = prefix_total * prefix_factor + suffix_total * suffix_factor
    attention = (
        (numerator / denominator[..., None])
        .reshape(own_rows, HEADS * HEAD_DIM)
        .astype(jnp.bfloat16)
    )
    attended = jnp.dot(
        lax.all_gather(attention, "ctx", axis=0, tiled=True),
        o_weight,
        preferred_element_type=jnp.float32,
    )
    mixed_rows = (tokens.astype(jnp.float32) + attended).astype(jnp.bfloat16)
    mlp_normed = normalized_rows(mixed_rows, mlp_gain)[0]
    gate_proj = jnp.dot(mlp_normed, gate_weight, preferred_element_type=jnp.float32)
    up_proj = jnp.dot(mlp_normed, up_weight, preferred_element_type=jnp.float32)
    hidden = (jax.nn.silu(gate_proj) * up_proj).astype(jnp.bfloat16)
    partial_value = jnp.dot(hidden, down_weight, preferred_element_type=jnp.float32)
    shares = lax.psum_scatter(partial_value, "ctx", scatter_dimension=1, tiled=True)
    return (mixed_rows.astype(jnp.float32) + shares).astype(jnp.bfloat16)


TOK, QRY, FRESH, PART, STAT, ATT, MIX, PAIR, DOWN, PHASES = range(10)
LANES = HEAD_DIM
GROUP = HEADS // KV_HEADS
FITS = 16


def regroup(rows, inner, outer):
    row = lax.broadcasted_iota(jnp.int32, (rows, rows), 0)
    column = lax.broadcasted_iota(jnp.int32, (rows, rows), 1)
    picked = (row % outer) * inner + row // outer
    return jnp.where(column == picked, 1.0, 0.0).astype(jnp.bfloat16)


def turn(block, cosine, signed_sine, even):
    swapped = jnp.where(even, pltpu.roll(block, LANES - 1, 1), pltpu.roll(block, 1, 1))
    return block * cosine + swapped * signed_sine


def layer_kernel(
    n,
    prefix_tokens,
    tokens,
    attn_gain,
    mlp_gain,
    q_hbm,
    k_hbm,
    v_hbm,
    o_hbm,
    gate_hbm,
    up_hbm,
    down_hbm,
    pk_hbm,
    pv_hbm,
    sk_hbm,
    sv_hbm,
    lengths,
    table,
    out,
    qw,
    kw,
    vw,
    ow,
    gw,
    uw,
    dw,
    pk,
    pv,
    sk,
    sv,
    again,
    mgain,
    tokbuf,
    qbuf,
    qperm,
    psend,
    precv,
    ssend,
    srecv,
    fsend,
    frecv,
    attbuf,
    mixbuf,
    dsend,
    dpair,
    drecv,
    load_sem,
    big_sem,
    send_sem,
    recv_sem,
):
    me = lax.axis_index("ctx")
    partner = me + 1 - 2 * (me % 2)
    half = n // 2
    core = me % 2
    chip = me // 2
    samples, width = tokens.shape
    ffn = gw.shape[1]
    scale = 1.0 / math.sqrt(HEAD_DIM)
    f32, bf16 = jnp.float32, jnp.bfloat16

    def load(source, target, index):
        return pltpu.make_async_copy(source, target, load_sem.at[index])

    def rows_of(d):
        return pl.ds(pl.multiple_of(d * width, width), width)

    def chunk(kind, d):
        if kind == 0:
            return pltpu.make_async_copy(q_hbm.at[rows_of(d)], qw.at[rows_of(d)], big_sem.at[0, d])
        if kind == 1:
            return pltpu.make_async_copy(o_hbm.at[rows_of(d)], ow.at[rows_of(d)], big_sem.at[1, d])
        if kind == 2:
            return pltpu.make_async_copy(
                gate_hbm.at[rows_of(d)], gw.at[rows_of(d)], big_sem.at[2, d]
            )
        return pltpu.make_async_copy(up_hbm.at[rows_of(d)], uw.at[rows_of(d)], big_sem.at[3, d])

    def down_chunk(step, target, place):
        d = 2 * ((chip + 1 + step) % half) + (core + 1 + step // half) % 2
        return pltpu.make_async_copy(
            down_hbm.at[:, rows_of(d)],
            target.at[pl.ds(pl.multiple_of(place * ffn, ffn), ffn)],
            big_sem.at[4, step],
        )

    def remote(phase, source, target, slot, landed, device):
        return pltpu.make_async_remote_copy(
            src_ref=source,
            dst_ref=target,
            send_sem=send_sem.at[phase, slot],
            recv_sem=recv_sem.at[phase, landed],
            device_id={"ctx": device},
            device_id_type=pl.DeviceIdType.MESH,
        )

    def loop(low, high, step):
        def wrapped(index, carry):
            step(index)
            return carry

        lax.fori_loop(low, high, wrapped, 0)

    def spread(phase, buf):
        loop(
            1,
            half,
            lambda k: remote(
                phase, buf.at[me], buf.at[me], k, me, (me + 2 * k) % n
            ).start(),
        )
        remote(phase, buf.at[me], buf.at[me], 0, me, partner).start()

    def relay(phase, buf, k):
        origin = (me + n - 2 * k) % n
        remote(phase, buf.at[origin], buf.at[origin], 0, origin, partner).wait_recv()
        remote(phase, buf.at[origin], buf.at[origin], half + k, origin, partner).start()
        return origin

    def arrive(phase, buf, k):
        origin = (partner + n - 2 * k) % n
        remote(phase, buf.at[origin], buf.at[origin], 0, origin, partner).wait_recv()
        return origin

    def collect(phase, buf):
        loop(1, half, functools.partial(relay, phase, buf))
        loop(0, half, functools.partial(arrive, phase, buf))

    def drain(phase, buf):
        def one(k):
            remote(phase, buf.at[me], buf.at[me], k, me, partner).wait_send()

        loop(0, half, one)
        loop(half + 1, n, one)

    def scatter_one(phase, source, target, k):
        device = (me + k) % n
        remote(phase, source.at[device], target.at[me], k, me, device).start()

    def gather_one(phase, source, target, k):
        origin = (me + n - k) % n
        remote(phase, source.at[origin], target.at[origin], k, origin, origin).wait_recv()

    def sent_one(phase, source, target, k):
        device = (me + k) % n
        remote(phase, source.at[device], target.at[me], k, me, device).wait_send()

    first = load(tokens, tokbuf.at[me], 0)
    first.start()
    small = [
        load(attn_gain, again, 1),
        load(mlp_gain, mgain, 2),
        load(k_hbm, kw, 3),
        load(v_hbm, vw, 4),
        load(pk_hbm, pk, 5),
        load(pv_hbm, pv, 6),
        load(sk_hbm, sk, 7),
        load(sv_hbm, sv, 8),
    ]
    barrier = pltpu.get_barrier_semaphore()
    loop(
        1,
        n,
        lambda k: pl.semaphore_signal(
            barrier,
            inc=1,
            device_id={"ctx": (me + k) % n},
            device_id_type=pl.DeviceIdType.MESH,
        ),
    )
    small[0].start()
    loop(0, n, lambda d: chunk(0, d).start())
    for copy in small[1:]:
        copy.start()
    first.wait()
    pl.semaphore_wait(barrier, n - 1)
    spread(TOK, tokbuf)
    loop(0, n, lambda d: chunk(1, d).start())

    def start_pair(d):
        chunk(2, d).start()
        chunk(3, d).start()

    loop(0, n, start_pair)
    loop(0, half, lambda i: down_chunk(i, dw, i).start())

    lane = lax.broadcasted_iota(jnp.int32, (samples, LANES), 1)
    row = lax.broadcasted_iota(jnp.int32, (samples, LANES), 0)
    even = lane % 2 == 0
    pair_index = (lane // 2).astype(f32)
    frequency = jnp.exp(pair_index * (-2.0 * math.log(ROPE_BASE) / HEAD_DIM))
    position = jnp.zeros((samples, LANES), jnp.int32)
    for s in range(samples):
        position = jnp.where(row == s, lengths[s] + prefix_tokens, position)
    angles = position.astype(f32) * frequency
    cosine = jnp.cos(angles)
    sine = jnp.where(even, -1.0, 1.0) * jnp.sin(angles)
    own_length = lengths[me]
    own_angles = (own_length + prefix_tokens).astype(f32) * frequency
    own_cosine = jnp.cos(own_angles)[:KV_HEADS]
    own_sine = (jnp.where(even, -1.0, 1.0) * jnp.sin(own_angles))[:KV_HEADS]
    to_sample = regroup(samples * GROUP, samples, GROUP)
    square = regroup(samples * samples, samples, samples)

    def inverse_root(buf):
        def add(d, total):
            block = buf[d].astype(f32)
            return total + jnp.sum(block * block, axis=1, keepdims=True)

        total = lax.fori_loop(0, n, add, jnp.zeros((samples, 1), f32), unroll=True)
        return lax.rsqrt(total / (n * width) + EPSILON)

    def normed(buf, root, gain, d):
        return (buf[d].astype(f32) * root * gain[:, rows_of(d)]).astype(bf16)

    for copy in small[:2]:
        copy.wait()
    collect(TOK, tokbuf)
    root = inverse_root(tokbuf)

    def q_step(d, total):
        chunk(0, d).wait()
        return total + jnp.dot(
            normed(tokbuf, root, again, d), qw[rows_of(d), :], preferred_element_type=f32
        )

    query = lax.fori_loop(0, n, q_step, jnp.zeros((samples, width), f32), unroll=4)
    for j in range(width // LANES):
        piece = slice(j * LANES, (j + 1) * LANES)
        qbuf[me, :, piece] = turn(query[:, piece], cosine, sine, even).astype(bf16)
    spread(QRY, qbuf)
    loop(half, n, lambda i: down_chunk(i, qw, i - half).start())

    for copy in small[2:]:
        copy.wait()
    mine = normed(tokbuf, root, again, me)
    terms = [
        jnp.dot(mine, kw[...], preferred_element_type=f32),
        jnp.dot(mine, vw[...], preferred_element_type=f32),
    ]
    stacked = jnp.concatenate(
        [
            term[:, c * LANES : (c + 1) * LANES]
            for term in terms
            for c in range(KV_HEADS)
        ],
        axis=0,
    )
    upper = stacked.astype(bf16)
    lower = (stacked - upper.astype(f32)).astype(bf16)
    by_owner = jnp.dot(square, upper, preferred_element_type=f32) + jnp.dot(
        square, lower, preferred_element_type=f32
    )
    by_owner = by_owner.reshape(n, 2 * KV_HEADS, LANES)
    fsend[...] = by_owner
    collect(QRY, qbuf)
    loop(1, n, lambda k: scatter_one(FRESH, fsend, frecv, k))
    frecv[me] = fsend[me]
    stat_lane = lax.broadcasted_iota(jnp.int32, (samples * GROUP, LANES), 1)
    stats = jnp.zeros((samples * GROUP, LANES), f32)
    per_device = width // LANES
    held = []
    for k in range(KV_HEADS):
        piece = slice(k * LANES, (k + 1) * LANES)
        heads = [k * GROUP + g for g in range(GROUP)]
        raw = jnp.concatenate(
            [
                qbuf[h // per_device, :, (h % per_device) * LANES : (h % per_device + 1) * LANES]
                for h in heads
            ],
            axis=0,
        )
        arranged = jnp.dot(to_sample, raw, preferred_element_type=f32)
        qperm[k] = arranged.astype(bf16).reshape(samples, GROUP, LANES)
        scores = (
            lax.dot_general(
                arranged.astype(bf16),
                pk[:, piece],
                (((1,), (1,)), ((), ())),
                preferred_element_type=f32,
            )
            * scale
        )
        peak = jnp.max(scores, axis=1, keepdims=True)
        weights = jnp.exp(scores - peak)
        total = jnp.sum(weights, axis=1, keepdims=True)
        summed = jnp.dot(weights.astype(bf16), pv[:, piece], preferred_element_type=f32)
        stats = jnp.where(stat_lane == k, peak, stats)
        stats = jnp.where(stat_lane == k + LANES // 2, total, stats)
        held.append(summed.reshape(samples, GROUP, LANES))
        if k % 2 == 1:
            psend[:, (k - 1) * GROUP : (k + 1) * GROUP, :] = jnp.concatenate(
                held, axis=1
            ).astype(bf16)
            held = []
    ssend[...] = stats.reshape(samples, GROUP, LANES)

    def send_part(k):
        scatter_one(STAT, ssend, srecv, k)
        scatter_one(PART, psend, precv, k)

    loop(1, n, send_part)
    srecv[me] = ssend[me]
    precv[me] = psend[me]

    loop(1, n, lambda k: gather_one(FRESH, fsend, frecv, k))
    fresh = lax.fori_loop(
        0, n, lambda d, total: total + frecv[d], jnp.zeros((2 * KV_HEADS, LANES), f32), unroll=True
    )
    fresh_keys = (
        turn(fresh[:KV_HEADS], own_cosine, own_sine, even[:KV_HEADS]).astype(bf16).astype(f32)
    )
    fresh_values = fresh[KV_HEADS:].astype(bf16).astype(f32)
    blocks, block = sk.shape[0], sk.shape[1]
    span = blocks * block
    place = lax.broadcasted_iota(jnp.int32, (GROUP, span), 1)
    slot = jnp.zeros((GROUP, span), jnp.int32)
    for i in range(blocks):
        slot = jnp.where(place // block == table[0, i], i * block + place % block, slot)
    live = slot < own_length
    own_lane = lax.broadcasted_iota(jnp.int32, (GROUP, LANES), 1)
    own_peaks = jnp.zeros((GROUP, LANES), f32)
    own_totals = jnp.zeros((GROUP, LANES), f32)
    own_sums = []
    for k in range(KV_HEADS):
        piece = slice(k * LANES, (k + 1) * LANES)
        mine_q = qperm[k, me].astype(f32)
        scores = (
            lax.dot_general(
                mine_q.astype(bf16),
                sk[:, :, piece].reshape(span, LANES),
                (((1,), (1,)), ((), ())),
                preferred_element_type=f32,
            )
            * scale
        )
        scores = jnp.where(live, scores, -1e30)
        fresh_score = (
            jnp.sum(mine_q * fresh_keys[k : k + 1], axis=1, keepdims=True) * scale
        )
        peak = jnp.maximum(jnp.max(scores, axis=1, keepdims=True), fresh_score)
        weights = jnp.where(live, jnp.exp(scores - peak), 0.0)
        fresh_weight = jnp.exp(fresh_score - peak)
        total = jnp.sum(weights, axis=1, keepdims=True) + fresh_weight
        summed = jnp.dot(
            weights.astype(bf16),
            sv[:, :, piece].reshape(span, LANES),
            preferred_element_type=f32,
        )
        own_sums.append(
            summed + fresh_weight.astype(bf16).astype(f32) * fresh_values[k : k + 1]
        )
        own_peaks = jnp.where(own_lane == k, peak, own_peaks)
        own_totals = jnp.where(own_lane == k, total, own_totals)

    loop(1, n, lambda k: gather_one(STAT, ssend, srecv, k))
    head_lane = own_lane < KV_HEADS
    best = lax.fori_loop(0, n, lambda d, top: jnp.maximum(top, srecv[d]), own_peaks, unroll=True)
    own_factor = jnp.exp(own_peaks - best)
    loop(1, n, lambda k: gather_one(PART, psend, precv, k))

    def column(tile):
        return jnp.concatenate(
            [
                jnp.broadcast_to(tile[:, k : k + 1], (GROUP, LANES))
                for k in range(KV_HEADS)
            ],
            axis=0,
        )

    def merge(d, carry):
        numerator, denominator = carry
        stat = srecv[d]
        factor = jnp.where(head_lane, jnp.exp(jnp.minimum(stat - best, 0.0)), 0.0)
        denominator = denominator + factor * pltpu.roll(stat, LANES // 2, 1)
        return numerator + column(factor) * precv[d].astype(f32), denominator

    numerator, denominator = lax.fori_loop(
        0,
        n,
        merge,
        (column(own_factor) * jnp.concatenate(own_sums, axis=0), own_factor * own_totals),
        unroll=2,
    )
    denominator = jnp.where(head_lane, denominator, 1.0)
    attbuf[me] = (numerator / column(denominator)).astype(bf16)
    spread(ATT, attbuf)
    drain(QRY, qbuf)
    collect(ATT, attbuf)
    for j in range(HEADS // samples):
        rows = attbuf[:, j * samples : (j + 1) * samples, :].reshape(samples * samples, LANES)
        swapped = jnp.dot(square, rows, preferred_element_type=f32).astype(bf16)
        for i in range(samples):
            h = j * samples + i
            qbuf[
                h // per_device, :, (h % per_device) * LANES : (h % per_device + 1) * LANES
            ] = swapped[i * samples : (i + 1) * samples]

    def o_step(d, total):
        chunk(1, d).wait()
        return total + jnp.dot(qbuf[d], ow[rows_of(d), :], preferred_element_type=f32)

    attended = lax.fori_loop(0, n, o_step, jnp.zeros((samples, width), f32), unroll=4)
    mixbuf[me] = (tokbuf[me].astype(f32) + attended).astype(bf16)
    spread(MIX, mixbuf)

    def ffn_step(d, carry):
        gate, up, squares = carry
        chunk(2, d).wait()
        chunk(3, d).wait()
        block = mixbuf[d].astype(f32)
        part = (block * mgain[:, rows_of(d)]).astype(bf16)
        gate = gate + jnp.dot(part, gw[rows_of(d), :], preferred_element_type=f32)
        up = up + jnp.dot(part, uw[rows_of(d), :], preferred_element_type=f32)
        return gate, up, squares + jnp.sum(block * block, axis=1, keepdims=True)

    zero = jnp.zeros((samples, ffn), f32)
    carry = ffn_step(me, (zero, zero, jnp.zeros((samples, 1), f32)))
    carry = lax.fori_loop(
        1, half, lambda k, c: ffn_step(relay(MIX, mixbuf, k), c), carry
    )
    gate, up, squares = lax.fori_loop(
        0, half, lambda k, c: ffn_step(arrive(MIX, mixbuf, k), c), carry, unroll=4
    )
    root = lax.rsqrt(squares / (n * width) + EPSILON)
    gate = gate * root
    up = up * root
    hidden = (gate / (1.0 + jnp.exp(-gate)) * up).astype(bf16)

    def down_step(step, weights, place):
        down_chunk(step, weights, place).wait()
        term = jnp.dot(
            hidden,
            weights[pl.ds(pl.multiple_of(place * ffn, ffn), ffn), :],
            preferred_element_type=f32,
        )
        return term

    def to_pair(c, slot):
        return remote(PAIR, dsend.at[c], dpair.at[c], slot, c, partner)

    def down_low(i, carry):
        c = (chip + 1 + i) % half
        dsend[c] = down_step(i, dw, i).astype(bf16)
        to_pair(c, i).start()
        return carry

    lax.fori_loop(0, half, down_low, 0, unroll=2)

    def to_chip(k):
        c = (chip + k) % half
        return remote(DOWN, dpair.at[c], drecv.at[chip], k, chip, 2 * c + core)

    def down_high(i, carry):
        c = (chip + 1 + i) % half
        term = down_step(half + i, qw, i)
        to_pair(c, 0).wait_recv()
        dpair[c] = (term + dpair[c].astype(f32)).astype(bf16)
        to_chip(i + 1).start()
        return carry

    lax.fori_loop(0, half - 1, down_high, 0)
    total = mixbuf[me].astype(f32) + down_step(n - 1, qw, half - 1)
    to_pair(chip, 0).wait_recv()
    total = total + dpair[chip].astype(f32)

    for phase, buf in ((TOK, tokbuf), (ATT, attbuf), (MIX, mixbuf)):
        drain(phase, buf)
    for phase, source, target in (
        (FRESH, fsend, frecv),
        (STAT, ssend, srecv),
        (PART, psend, precv),
    ):
        loop(1, n, functools.partial(sent_one, phase, source, target))

    def finish(k, total):
        origin = (chip + half - k) % half
        remote(
            DOWN, dpair.at[origin], drecv.at[origin], 0, origin, 2 * origin + core
        ).wait_recv()
        return total + drecv[origin].astype(f32)

    total = lax.fori_loop(1, half, finish, total)
    out[...] = total.astype(bf16)
    loop(0, half, lambda i: to_pair((chip + 1 + i) % half, i).wait_send())
    loop(1, half, lambda k: to_chip(k).wait_send())


def body(*args):
    tokens, q_weight, gate_weight = args[0], args[3], args[7]
    prefix_keys, suffix_keys, suffix_table = args[10], args[12], args[15]
    n = lax.axis_size("ctx")
    samples, width = tokens.shape
    ffn = gate_weight.shape[1]
    fits = (
        samples == n == FITS == 2 * KV_HEADS
        and suffix_table.shape[0] == 1
        and width % LANES == 0
        and n * width == HEADS * HEAD_DIM
        and q_weight.shape[0] == (n // 2) * ffn
        and suffix_keys.shape[0] * suffix_keys.shape[1] == LANES
    )
    if not fits:
        return plain_body(*args)
    args = list(args)
    args[1] = args[1].reshape(1, -1)
    args[2] = args[2].reshape(1, -1)
    bf16, f32 = jnp.bfloat16, jnp.float32
    kept = [args[i] for i in (3, 4, 5, 6, 7, 8)]
    exchange = pltpu.VMEM((n, samples, width), bf16)
    parts = pltpu.VMEM((n, HEADS, LANES), bf16)
    stats = pltpu.VMEM((n, GROUP, LANES), f32)
    fresh = pltpu.VMEM((n, 2 * KV_HEADS, LANES), f32)
    anywhere = pl.BlockSpec(memory_space=pl.ANY)
    scalars = pl.BlockSpec(memory_space=pltpu.SMEM)
    return pl.pallas_call(
        functools.partial(layer_kernel, n, prefix_keys.shape[0] * n),
        out_shape=jax.ShapeDtypeStruct((samples, width), bf16),
        in_specs=[anywhere] * 14 + [scalars] * 2,
        out_specs=pl.BlockSpec(memory_space=pltpu.VMEM),
        scratch_shapes=[pltpu.VMEM(w.shape, bf16) for w in kept]
        + [pltpu.VMEM(((n // 2) * ffn, width), bf16)]
        + [pltpu.VMEM(args[i].shape, bf16) for i in (10, 11, 12, 13)]
        + [pltpu.VMEM((1, n * width), f32)] * 2
        + [
            exchange,
            exchange,
            pltpu.VMEM((KV_HEADS, samples, GROUP, LANES), bf16),
            parts,
            parts,
            stats,
            stats,
            fresh,
            fresh,
            parts,
            exchange,
            pltpu.VMEM((n // 2, samples, width), bf16),
            pltpu.VMEM((n // 2, samples, width), bf16),
            pltpu.VMEM((n // 2, samples, width), bf16),
            pltpu.SemaphoreType.DMA((9,)),
            pltpu.SemaphoreType.DMA((5, n)),
            pltpu.SemaphoreType.DMA((PHASES, n)),
            pltpu.SemaphoreType.DMA((PHASES, n)),
        ],
        compiler_params=pltpu.CompilerParams(
            collective_id=0, has_side_effects=True, vmem_limit_bytes=67043328
        ),
        name="layer",
    )(*args)


def solution(mesh):
    placed = (
        P("groups", "ctx"),
        P(),
        P(),
        P(None, "ctx"),
        P("ctx", None),
        P("ctx", None),
        P(None, "ctx"),
        P(None, "ctx"),
        P(None, "ctx"),
        P("ctx", None),
        P(("groups", "ctx"), None),
        P(("groups", "ctx"), None),
        P(("groups", "ctx"), None, None),
        P(("groups", "ctx"), None, None),
        P("groups"),
        P(("groups", "ctx"), None),
    )
    return jax.shard_map(
        body, mesh=mesh, in_specs=placed, out_specs=P("groups", "ctx"), check_vma=False
    )
```
